256 devices in a mesh: tm: 32 (over z, y), state: 8 (over x, core).
Axes of the slice: x: 4, y: 4, z: 8, core: 2. Of those that a mesh axis runs over, the one named last changes fastest.
Arguments:
- inputs: bfloat16 [4, 4096, 256], P(None, 'tm'), may hold values from -6 to 6
- encoder_in: bfloat16 [256, 2048], P(None, 'state'), may hold values from -0.375 to 0.375
- encoder_out: bfloat16 [2048, 1024], P('state'), may hold values from -0.125 to 0.125
- readings: bfloat16 [4, 4096, 8192], P(None, 'tm', 'state'), may hold values from -6 to 6
- available: int32 [4, 4096, 64], P(None, 'tm', 'state'), may hold values 0 or 1
- pattern: int32 [64, 4], P('state'), may hold values from 0 to 7, all different within a row
- gain_blocks: bfloat16 [64, 4, 128, 128], P('state'), may hold values from -0.109375 to 0.109375
- load_blocks: bfloat16 [64, 4, 128, 128], P('state'), may hold values from -0.25 to 0.25
- retain: float32 [1024, 4, 4096], P('state', None, 'tm'), may hold values from 0.1 to 1
- smooth: float32 [1024, 4, 4096], P('state', None, 'tm'), may hold values from 0.1 to 1
- cotangent: bfloat16 [4, 4096, 8192], P(None, 'tm', 'state'), may hold values from -6 to 6
Outputs:
- predicted: bfloat16 [4, 4096, 8192], P(None, 'tm', 'state')
- sensor_grad: bfloat16 [4, 4096, 8192], P(None, 'tm', 'state')
The draws below stay inside these ranges and needn't reach their ends.
Inputs may be any that keep to these rules, and one draw needn't show every extreme that they name: `pattern`: row q lists 4 different state blocks read by sensor block q; every state block appears in some row.
All inputs are finite; a program needn't handle non-finite values. No bound on the sum of `available` on one device may be relied on, other than what follows from the above.
Results may differ from the reference program's by a relative error of at most 0.005.
Values may be sent and summed in bfloat16 or wider, within the bound.
No kernel may reach another device: no remote copies, remote signals or barrier semaphores. Data moves between devices by JAX's collectives and lax.ppermute only.
A program may use at most 128 MiB of HBM per device.

```python
import jax
import jax.numpy as jnp
from jax import lax

S = 1024
SENS = 8192
BLK = 128
NB = 4
FEAT = 256
HID = 2048
BATCH = 4
T_SIZE = 4096
SB = 64


def decay_law(key, fast_share):
    keys = jax.random.split(key, 6)
    fast = jax.random.bernoulli(keys[0], fast_share, (S,)).astype(jnp.float32)
    life = jax.random.uniform(keys[1], (S,), jnp.float32, 30.0, 60.0)
    slow_rate = -jnp.log(0.8) / T_SIZE * jax.random.uniform(keys[2], (S,), jnp.float32, 0.5, 1.5)
    rate = fast * (3.0 / life) + (1.0 - fast) * slow_rate
    jitter = jax.random.uniform(keys[3], (S, BATCH, T_SIZE), jnp.float32, 0.5, 1.5)
    starting_offset = jnp.exp(-rate[:, None, None] * jitter)
    places = jax.random.randint(keys[4], (BATCH, 3), 0, T_SIZE)
    nesting_levels = jax.random.uniform(keys[5], (BATCH, 3), jnp.float32, 0.55, 0.8)
    match_count = jnp.arange(T_SIZE)[None, None, :] == places[:, :, None]
    spike_amplitude = jnp.prod(jnp.where(match_count, nesting_levels[:, :, None], 1.0), axis=1)
    return starting_offset * spike_amplitude[None, :, :]


def draw_retain(key, part):
    share = 0.5
    return decay_law(jax.random.fold_in(key, 11), share)


def draw_smooth(key, part):
    share = 0.5
    return decay_law(jax.random.fold_in(key, 23), share)


def plant(array, key, least, high):
    shape = array.shape
    spot = [jax.random.randint(jax.random.fold_in(key, axis), (), 0, shape[axis]) for axis in range(len(shape))]
    array = array.at[tuple(spot)].set(least)
    longest = shape.index(max(shape))
    spot[longest] = (spot[longest] + 1) % shape[longest]
    return array.at[tuple(spot)].set(high)


def level_of(rng, dims, cuts, smallest, largest):
    gain, own = 1.0, jax.random.fold_in(rng, 6)
    for dim, shards_of in cuts:
        draws = jnp.exp(jax.random.uniform(jax.random.fold_in(own, dim), (shards_of,), jnp.float32, smallest / len(cuts), largest / len(cuts)))
        gain = gain * jnp.repeat(draws, dims[dim] // shards_of).reshape([-1 if axis == dim else 1 for axis in range(len(dims))])
    return gain


def picks_of(own_key, rows, number_of, top, lift):
    order = jax.random.permutation(jax.random.fold_in(own_key, 1), number_of)
    pull = order
    for power in range(3):
        pull = pull * pull // number_of
    pull = pull * lift // number_of
    tickets = jax.random.randint(jax.random.fold_in(own_key, 2), (rows, number_of), 0, 4096) + pull
    holders = jax.random.permutation(jax.random.fold_in(own_key, 3), rows)[jnp.arange(number_of) % rows]
    tickets = jnp.where(jnp.arange(rows)[:, None] == holders[None, :], 1 << 14, tickets)
    merit = tickets * number_of + jnp.arange(number_of)
    return lax.top_k(merit.astype(jnp.int32), top)[1].astype(jnp.int32)


def bell_draw(rng, shape, deviation, limit, pieces=(), kind=jnp.bfloat16):
    array = jax.random.normal(rng, shape, jnp.float32) * deviation
    if len(pieces) > 0:
        array = level_of(rng, shape, pieces, -0.22, 0.18) * array
    return jnp.clip(array, min=-limit, max=limit).astype(kind)


def setup_inputs(seed: int = 0) -> dict:
    streams_of = jax.random.split(jax.random.key(seed), 12)
    return {
        "inputs": bell_draw(streams_of[0], (BATCH, T_SIZE, FEAT), 1.0, 6.0, ((1, 32),)),
        "encoder_in": bell_draw(streams_of[1], (FEAT, HID), FEAT ** -0.5, 0.375, ((1, 8),)),
        "encoder_out": bell_draw(streams_of[2], (HID, S), HID ** -0.5, 0.125, ((0, 8),)),
        "readings": bell_draw(streams_of[3], (BATCH, T_SIZE, SENS), 1.0, 6.0, ((1, 32), (2, 8))),
        "available": plant((jax.random.randint(streams_of[4], (BATCH, T_SIZE, SB), 0, 4) < 3).astype(jnp.int32), jax.random.fold_in(streams_of[4], 1), 0, 1),
        "pattern": picks_of(streams_of[5], SB, S // BLK, NB, 0),
        "gain_blocks": bell_draw(streams_of[6], (SB, NB, BLK, BLK), (3 * SENS * NB * BLK // (4 * S)) ** -0.5, 0.109375, ((0, 8),)),
        "load_blocks": bell_draw(streams_of[7], (SB, NB, BLK, BLK), (NB * BLK) ** -0.5, 0.25, ((0, 8),)),
        "retain": draw_retain(jax.random.fold_in(streams_of[11], 71), 0),
        "smooth": draw_smooth(jax.random.fold_in(streams_of[11], 71), 0),
        "cotangent": bell_draw(streams_of[10], (BATCH, T_SIZE, SENS), 1.0, 6.0, ((1, 32), (2, 8))),
    }


def to_time(matrix):
    return matrix.reshape(BATCH, T_SIZE, S).transpose(1, 0, 2)

def to_rows(matrix):
    return matrix.transpose(1, 0, 2).reshape(BATCH * T_SIZE, S)

def filter_step(memory, pair_in):
    factor, source = pair_in
    updated = factor * memory + source
    return (updated, updated)

def ahead_step(memory, pair_in):
    factor, source = pair_in
    return (factor * memory + source, memory)

def carry_step(memory, pair_in):
    factor, source = pair_in
    return (factor * (memory + source), memory)

def reference(inputs, encoder_in, encoder_out, readings, available, pattern, gain_blocks, load_blocks, retain, smooth, cotangent):
    row_total = BATCH * T_SIZE
    hidden = jax.nn.gelu(jnp.dot(inputs.reshape(row_total, FEAT), encoder_in, preferred_element_type=jnp.float32)).astype(jnp.bfloat16)
    encoded = jnp.dot(hidden, encoder_out, preferred_element_type=jnp.float32)
    mask_rows = available.reshape(row_total, SB)
    observed = readings.reshape(row_total, SB, BLK) * mask_rows.reshape(row_total, SB, 1).astype(jnp.bfloat16)
    cot_blocks = cotangent.reshape(row_total, SB, BLK)

    def add_block(block_index, partial_value):
        drive_sum, pull_sum = partial_value
        block_id = block_index.astype(jnp.int32)
        obs_here = lax.dynamic_index_in_dim(observed, block_id, 1, keepdims=False)
        cot_here = lax.dynamic_index_in_dim(cot_blocks, block_id, 1, keepdims=False)
        targets = lax.dynamic_index_in_dim(pattern, block_id, 0, keepdims=False)
        gain_here = lax.dynamic_index_in_dim(gain_blocks, block_id, 0, keepdims=False)
        current_load = lax.dynamic_index_in_dim(load_blocks, block_id, 0, keepdims=False)
        for column in range(NB):
            offset = (targets[column] * BLK).astype(jnp.int32)
            pushed = jnp.dot(obs_here, gain_here[column], preferred_element_type=jnp.float32)
            pulled = jnp.dot(cot_here, current_load[column].T, preferred_element_type=jnp.float32)
            drive_sum = lax.dynamic_update_slice_in_dim(drive_sum, lax.dynamic_slice_in_dim(drive_sum, offset, BLK, 1) + pushed, offset, 1)
            pull_sum = lax.dynamic_update_slice_in_dim(pull_sum, lax.dynamic_slice_in_dim(pull_sum, offset, BLK, 1) + pulled, offset, 1)
        return (drive_sum, pull_sum)
    drive_in, pull_in = lax.fori_loop(0, SB, add_block, (encoded, jnp.zeros((row_total, S), jnp.float32)))
    drive_time = to_time(drive_in)
    pull_time = to_time(pull_in)
    retain_t = retain.transpose(2, 1, 0)
    smooth_t = smooth.transpose(2, 1, 0)
    gain_root = jnp.sqrt(1.0 - retain_t * retain_t)
    innovation = gain_root * drive_time
    zero_state = jnp.zeros((BATCH, S), jnp.float32)
    _, filtered = lax.scan(filter_step, zero_state, (retain_t, innovation))
    _, ahead_next = lax.scan(ahead_step, zero_state, (smooth_t, innovation), reverse=True)
    smoothed = filtered + smooth_t * ahead_next
    _, rise_prev = lax.scan(carry_step, zero_state, (smooth_t, pull_time))
    _, fall_next = lax.scan(carry_step, zero_state, (retain_t, pull_time), reverse=True)
    adjoint = pull_time + fall_next + rise_prev
    drive_grad = to_rows((gain_root * adjoint).astype(jnp.bfloat16))
    states_bf = to_rows(smoothed.astype(jnp.bfloat16))

    def project_block(block_index):
        block_id = block_index.astype(jnp.int32)
        targets = lax.dynamic_index_in_dim(pattern, block_id, 0, keepdims=False)
        gain_here = lax.dynamic_index_in_dim(gain_blocks, block_id, 0, keepdims=False)
        current_load = lax.dynamic_index_in_dim(load_blocks, block_id, 0, keepdims=False)
        mask_here = lax.dynamic_index_in_dim(mask_rows, block_id, 1, keepdims=True).astype(jnp.float32)
        predicted = jnp.zeros((row_total, BLK), jnp.float32)
        backpropagated_value = jnp.zeros((row_total, BLK), jnp.float32)
        for column in range(NB):
            offset = (targets[column] * BLK).astype(jnp.int32)
            predicted = predicted + jnp.dot(lax.dynamic_slice_in_dim(states_bf, offset, BLK, 1), current_load[column], preferred_element_type=jnp.float32)
            backpropagated_value = backpropagated_value + jnp.dot(lax.dynamic_slice_in_dim(drive_grad, offset, BLK, 1), gain_here[column].T, preferred_element_type=jnp.float32)
        return (predicted.astype(jnp.bfloat16), (backpropagated_value * mask_here).astype(jnp.bfloat16))
    preds, grads = lax.map(project_block, jnp.arange(SB, dtype=jnp.int32))
    predicted = preds.transpose(1, 0, 2).reshape(BATCH, T_SIZE, SENS)
    sensor_grad = grads.transpose(1, 0, 2).reshape(BATCH, T_SIZE, SENS)
    return (predicted, sensor_grad)
```

```python
import functools

import jax
import jax.numpy as jnp
from jax import lax
from jax.experimental import pallas as pl
from jax.experimental.pallas import tpu as pltpu
from jax.sharding import PartitionSpec as P


F32, BF16 = jnp.float32, jnp.bfloat16
VMEM = 16 << 20
BLK = 128
SEG = 8
NT = (((1,), (1,)), ((), ()))
NN = (((1,), (0,)), ((), ()))


def call(kernel, outs, operands, scratch=(), smem=0, flops=0):
    vmem, scalar = pl.BlockSpec(memory_space=pltpu.VMEM), pl.BlockSpec(memory_space=pltpu.SMEM)
    moved = sum(a.size * a.dtype.itemsize for a in (*operands, *outs))
    return pl.pallas_call(
        kernel,
        out_shape=outs,
        in_specs=[scalar] * smem + [vmem] * (len(operands) - smem),
        out_specs=tuple([vmem] * len(outs)),
        scratch_shapes=list(scratch),
        compiler_params=pltpu.CompilerParams(vmem_limit_bytes=VMEM),
        cost_estimate=pl.CostEstimate(flops=flops, bytes_accessed=moved, transcendentals=0),
    )(*operands)


def struct(shape, dtype):
    return jax.ShapeDtypeStruct(shape, dtype)


def split_blocks(place, total, at, keep, send):
    x, core = place[0], place[1]
    slot = lax.rem(at - x + 4, 4)
    low, high = total[:, :BLK], total[:, BLK:]
    mine = core == 0
    keep[slot] = jnp.where(mine, low, high)
    send[slot] = jnp.where(mine, high, low).astype(BF16)


def drive_kernel(place, pattern, rows_in, enc_in, enc_out, readings, mask, gain, weights, keep, send, lhs):
    blocks, reads = gain.shape[0], gain.shape[1]
    weights[...] = jnp.zeros_like(weights)
    for q in range(blocks):
        for k in range(reads):
            column = pl.multiple_of(pattern[q, k] * BLK, BLK)
            weights[q * BLK : (q + 1) * BLK, pl.ds(column, BLK)] = gain[q, k]
        lhs[:, q * BLK : (q + 1) * BLK] = readings[:, q * BLK : (q + 1) * BLK] * mask[:, q : q + 1].astype(BF16)
    hidden = jax.nn.gelu(jnp.dot(rows_in[...], enc_in[...], preferred_element_type=F32)).astype(BF16)

    def columns(at, _):
        window = pl.ds(pl.multiple_of(at * 2 * BLK, 2 * BLK), 2 * BLK)
        total = jnp.dot(lhs[...], weights[:, window], preferred_element_type=F32)
        total += jnp.dot(hidden, enc_out[:, window], preferred_element_type=F32)
        split_blocks(place, total, at, keep, send)
        return 0

    lax.fori_loop(0, 4, columns, 0)


def pull_kernel(place, pattern, cotangent, load, weights, keep, send):
    blocks, reads = load.shape[0], load.shape[1]
    weights[...] = jnp.zeros_like(weights)
    for q in range(blocks):
        for k in range(reads):
            row = pl.multiple_of(pattern[q, k] * BLK, BLK)
            weights[pl.ds(row, BLK), q * BLK : (q + 1) * BLK] = load[q, k]

    def columns(at, _):
        window = pl.ds(pl.multiple_of(at * 2 * BLK, 2 * BLK), 2 * BLK)
        total = lax.dot_general(cotangent[...], weights[window, :], NT, preferred_element_type=F32)
        split_blocks(place, total, at, keep, send)
        return 0

    lax.fori_loop(0, 4, columns, 0)


def merge_kernel(keep, came, own, *pieces):
    own[...] = keep[0] + came[0].astype(F32)
    for k, piece in enumerate(pieces):
        piece[...] = (keep[k + 1] + came[k + 1].astype(F32)).astype(BF16)


def rows_of(b, u, steps):
    return pl.ds(b * steps + u, SEG, stride=steps // SEG)


def turn(x, by, fill, backward):
    row = lax.broadcasted_iota(jnp.int32, x.shape, 0)
    if backward:
        return jnp.where(row < SEG - by, pltpu.roll(x, SEG - by, 0), fill)
    return jnp.where(row >= by, pltpu.roll(x, by, 0), fill)


def chain(factor, value, backward):
    for by in (1, 2, 4):
        value = factor * turn(value, by, 0.0, backward) + value
        factor = factor * turn(factor, by, 1.0, backward)
    return factor, value, turn(factor, 1, 1.0, backward), turn(value, 1, 0.0, backward)


def decay_kernel(traces, steps, retain, smooth, keep_r, keep_s, root, ahead_p, filt_p, rise_p, fall_p, seg_r, seg_s):
    for b in range(traces):
        span = slice(b * steps, (b + 1) * steps)
        keep_r[span, :] = retain[pl.ds(b, BLK, stride=traces), :].T
        keep_s[span, :] = smooth[pl.ds(b, BLK, stride=traces), :].T
    root[...] = jnp.sqrt(1.0 - keep_r[...] * keep_r[...])
    ones = jnp.ones((SEG, BLK), F32)
    for b in range(traces):
        filt, rise = ones, ones
        for u in range(steps // SEG):
            at = rows_of(b, u, steps)
            r, s = keep_r[at, :], keep_s[at, :]
            filt = filt * r
            filt_p[at, :] = filt
            rise_p[at, :] = rise
            rise = rise * s
        seg_r[b] = filt
        seg_s[b] = rise
        ahead, fall = ones, ones
        for u in reversed(range(steps // SEG)):
            at = rows_of(b, u, steps)
            r, s = keep_r[at, :], keep_s[at, :]
            ahead = ahead * s
            ahead_p[at, :] = ahead
            fall_p[at, :] = fall
            fall = fall * r


def scan_kernel(
    traces, steps, place,
    own_a, a1, a2, a3, own_b, b1, b2, b3, keep_r, keep_s, root, seg_r, seg_s,
    states, grads, before, parcel,
    source, pull, ends,
):
    source[...] = root[...] * (own_a[...] + a1[...].astype(F32) + a2[...].astype(F32) + a3[...].astype(F32))
    pull[...] = own_b[...] + b1[...].astype(F32) + b2[...].astype(F32) + b3[...].astype(F32)
    for b in range(traces):
        filt = jnp.zeros((SEG, BLK), F32)
        rise, ahead, fall = filt, filt, filt
        for u in range(steps // SEG):
            at = rows_of(b, u, steps)
            r, s, g, p = keep_r[at, :], keep_s[at, :], source[at, :], pull[at, :]
            filt = r * filt + g
            states[at, :] = filt
            carried = rise + p
            grads[at, :] = carried
            rise = s * carried
        for u in reversed(range(steps // SEG)):
            at = rows_of(b, u, steps)
            r, s, g, p = keep_r[at, :], keep_s[at, :], source[at, :], pull[at, :]
            later = s * ahead
            states[at, :] = states[at, :] + later
            ahead = later + g
            grads[at, :] = grads[at, :] + fall
            fall = r * (fall + p)
        for which, (factor, value, backward) in enumerate(
            ((seg_r[b], filt, False), (seg_s[b], rise, False), (seg_s[b], ahead, True), (seg_r[b], fall, True))
        ):
            whole, total, factor_before, value_before = chain(factor, value, backward)
            before[which, b, 0] = factor_before
            before[which, b, 1] = value_before
            end = 0 if backward else SEG - 1
            half, row = which // 2, (which % 2) * traces + b
            ends[half, 0, row : row + 1, :] = total[end : end + 1, :]
            ends[half, 1, row : row + 1, :] = whole[end : end + 1, :]
    me = place[2]
    for target in range(parcel.shape[0]):
        onward = target > me
        parcel[target, :SEG] = jnp.where(onward, ends[0, 0], ends[1, 0])
        parcel[target, SEG:] = jnp.where(onward, ends[0, 1], ends[1, 1])


def settle_kernel(
    traces, steps, place,
    parcel, before, states, grads, root, ahead_p, filt_p, rise_p, fall_p,
    states_bf, grads_bf,
    sums, carry,
):
    me, length = place[2], parcel.shape[0]
    onward = jnp.zeros((SEG, BLK), F32)
    back = onward
    for j in range(length):
        onward = jnp.where(j < me, parcel[j, SEG:] * onward + parcel[j, :SEG], onward)
        i = length - 1 - j
        back = jnp.where(i > me, parcel[i, SEG:] * back + parcel[i, :SEG], back)
    carry[0] = onward
    carry[1] = back
    for b in range(traces):
        filt, rise, ahead, fall = (
            before[w, b, 1] + before[w, b, 0] * carry[w // 2, (w % 2) * traces + b : (w % 2) * traces + b + 1, :]
            for w in range(4)
        )
        for u in range(steps // SEG):
            at = rows_of(b, u, steps)
            sums[0, at, :] = states[at, :] + filt_p[at, :] * filt + ahead_p[at, :] * ahead
            sums[1, at, :] = root[at, :] * (grads[at, :] + rise_p[at, :] * rise + fall_p[at, :] * fall)
    states_bf[...] = sums[0].astype(BF16)
    grads_bf[...] = sums[1].astype(BF16)


def project_kernel(dims, masked, place, *refs):
    *pieces, weights, mask, out, lhs = refs
    x, core = place[0], place[1]
    for k in range(4):
        column = 2 * lax.rem(x - k + 4, 4)
        for side in range(2):
            block = column + (core if side == 0 else 1 - core)
            lhs[:, pl.ds(pl.multiple_of(block * BLK, BLK), BLK)] = pieces[side * 4 + k][...]
    for at in range(4):
        window = slice(at * 2 * BLK, (at + 1) * 2 * BLK)
        chosen = weights[window, :] if dims is NT else weights[:, window]
        total = lax.dot_general(lhs[...], chosen, dims, preferred_element_type=F32)
        for half in range(2):
            q = 2 * at + half
            piece = total[:, half * BLK : (half + 1) * BLK]
            if masked:
                piece = piece * mask[:, q : q + 1].astype(F32)
            out[:, q * BLK : (q + 1) * BLK] = piece.astype(BF16)


def local(inputs, encoder_in, encoder_out, readings, available, pattern, gain, load, retain, smooth, cotangent):
    traces, steps, features = inputs.shape
    rows = traces * steps
    sensors, hidden = readings.shape[2], encoder_in.shape[1]
    states = encoder_out.shape[1]
    axis, times = lax.axis_size("state"), lax.axis_size("tm")
    at = lax.axis_index("state")
    place = jnp.stack([at // 2, at % 2, lax.axis_index("tm")]).astype(jnp.int32)
    swap = [(i, i ^ 1) for i in range(axis)]
    shift = {k: [(i, (i + 2 * k) % axis) for i in range(axis)] for k in (1, 2, 3)}
    mask = available.reshape(rows, -1)
    work = 2 * rows * sensors * states

    gain_weights, keep_a, send_a = call(
        drive_kernel,
        (struct((sensors, states), BF16), struct((4, rows, BLK), F32), struct((4, rows, BLK), BF16)),
        (place, pattern, inputs.reshape(rows, features), encoder_in, encoder_out, readings.reshape(rows, sensors), mask, gain),
        scratch=[pltpu.VMEM((rows, sensors), BF16)],
        smem=2,
        flops=work,
    )
    came_a = lax.ppermute(send_a, "state", swap)
    load_weights, keep_b, send_b = call(
        pull_kernel,
        (struct((states, sensors), BF16), struct((4, rows, BLK), F32), struct((4, rows, BLK), BF16)),
        (place, pattern, cotangent.reshape(rows, sensors), load),
        smem=2,
        flops=work,
    )
    came_b = lax.ppermute(send_b, "state", swap)
    pieces = (struct((rows, BLK), F32),) + (struct((rows, BLK), BF16),) * 3
    own_a, *out_a = call(merge_kernel, pieces, (keep_a, came_a))
    in_a = [lax.ppermute(piece, "state", shift[k + 1]) for k, piece in enumerate(out_a)]
    own_b, *out_b = call(merge_kernel, pieces, (keep_b, came_b))
    in_b = [lax.ppermute(piece, "state", shift[k + 1]) for k, piece in enumerate(out_b)]

    full, segments = struct((rows, BLK), F32), struct((traces, SEG, BLK), F32)
    keep_r, keep_s, root, ahead_p, filt_p, rise_p, fall_p, seg_r, seg_s = call(
        functools.partial(decay_kernel, traces, steps),
        (full,) * 7 + (segments,) * 2,
        (retain.reshape(-1, steps), smooth.reshape(-1, steps)),
    )
    scanned, pulled, before, parcel = call(
        functools.partial(scan_kernel, traces, steps),
        (full, full, struct((4, traces, 2, SEG, BLK), F32), struct((times, 2 * SEG, BLK), F32)),
        (place, own_a, *in_a, own_b, *in_b, keep_r, keep_s, root, seg_r, seg_s),
        scratch=[pltpu.VMEM((rows, BLK), F32)] * 2 + [pltpu.VMEM((2, 2, SEG, BLK), F32)],
        smem=1,
    )
    parcel = lax.all_to_all(parcel, "tm", 0, 0)
    half = struct((rows, BLK), BF16)
    states_bf, grads_bf = call(
        functools.partial(settle_kernel, traces, steps),
        (half, half),
        (place, parcel, before, scanned, pulled, root, ahead_p, filt_p, rise_p, fall_p),
        scratch=[pltpu.VMEM((2, rows, BLK), F32), pltpu.VMEM((2, SEG, BLK), F32)],
        smem=1,
    )

    def everyone(piece):
        same = [piece] + [lax.ppermute(piece, "state", shift[k]) for k in (1, 2, 3)]
        return same + [lax.ppermute(one, "state", swap) for one in same]

    all_states, all_grads = everyone(states_bf), everyone(grads_bf)
    out = (struct((rows, sensors), BF16),)
    scratch = [pltpu.VMEM((rows, states), BF16)]
    (predicted,) = call(
        functools.partial(project_kernel, NN, False), out, (place, *all_states, load_weights, mask), scratch, 1, work
    )
    (sensor_grad,) = call(
        functools.partial(project_kernel, NT, True), out, (place, *all_grads, gain_weights, mask), scratch, 1, work
    )
    return predicted.reshape(readings.shape), sensor_grad.reshape(readings.shape)


def solution(mesh):
    placed = (
        P(None, "tm", None),
        P(None, "state"),
        P("state", None),
        P(None, "tm", "state"),
        P(None, "tm", "state"),
        P("state", None),
        P("state", None, None, None),
        P("state", None, None, None),
        P("state", None, "tm"),
        P("state", None, "tm"),
        P(None, "tm", "state"),
    )
    return jax.shard_map(
        local,
        mesh=mesh,
        in_specs=placed,
        out_specs=(P(None, "tm", "state"), P(None, "tm", "state")),
        check_vma=False,
    )
```

```python
import functools

import jax
import jax.numpy as jnp
from jax import lax
from jax.experimental import pallas as pl
from jax.experimental.pallas import tpu as pltpu
from jax.sharding import PartitionSpec as P


F32, BF16 = jnp.float32, jnp.bfloat16
VMEM = 20 << 20
BLK = 128
SEG = 8
NT = (((1,), (1,)), ((), ()))
NN = (((1,), (0,)), ((), ()))


def call(kernel, outs, operands, scratch=(), smem=0, hbm=0, hbm_out=False, flops=0):
    vmem, scalar = pl.BlockSpec(memory_space=pltpu.VMEM), pl.BlockSpec(memory_space=pltpu.SMEM)
    far = pl.BlockSpec(memory_space=pltpu.HBM)
    moved = sum(a.size * a.dtype.itemsize for a in (*operands, *outs))
    return pl.pallas_call(
        kernel,
        out_shape=outs,
        in_specs=[scalar] * smem + [vmem] * (len(operands) - smem - hbm) + [far] * hbm,
        out_specs=tuple([far if hbm_out else vmem] * len(outs)),
        scratch_shapes=list(scratch),
        compiler_params=pltpu.CompilerParams(vmem_limit_bytes=VMEM),
        cost_estimate=pl.CostEstimate(flops=flops, bytes_accessed=moved, transcendentals=0),
    )(*[pltpu.with_memory_space_constraint(a, pltpu.HBM) if i >= len(operands) - hbm else a for i, a in enumerate(operands)])


def struct(shape, dtype):
    return jax.ShapeDtypeStruct(shape, dtype)


def front_kernel(
    place, pattern, available, load_far, cot_far, gain_far, readings_far, rows_far, enc_in_far, enc_out_far,
    load_weights, gain_weights, keep, send, mask,
    load, cotangent, gain, lhs, rows_in, enc_in, enc_out, sems,
):
    core = place[1]
    pairs = (
        (load_far, load), (cot_far, cotangent), (gain_far, gain), (readings_far, lhs),
        (rows_far, rows_in), (enc_in_far, enc_in), (enc_out_far, enc_out),
    )
    copies = [pltpu.make_async_copy(far, near, sems.at[i]) for i, (far, near) in enumerate(pairs)]
    for copy in copies:
        copy.start()
    load_weights[...] = jnp.zeros_like(load_weights)
    gain_weights[...] = jnp.zeros_like(gain_weights)
    traces, blocks, steps = available.shape
    reads = pattern.shape[0]
    for b in range(traces):
        mask[b * steps : (b + 1) * steps, :] = available[b].astype(F32).T

    def split(which, at, total):
        low, high = total[:, :BLK], total[:, BLK:]
        keep[at, which] = jnp.where(core == 0, low, high)
        send[at, which] = jnp.where(core == 0, high, low).astype(BF16)

    copies[0].wait()
    for q in range(blocks):
        for k in range(reads):
            row = pl.multiple_of(pattern[k, q] * BLK, BLK)
            load_weights[pl.ds(row, BLK), q * BLK : (q + 1) * BLK] = load[q, k]
    copies[1].wait()

    def pull_columns(at, _):
        window = pl.ds(pl.multiple_of(at * 2 * BLK, 2 * BLK), 2 * BLK)
        split(1, at, lax.dot_general(cotangent[...], load_weights[window, :], NT, preferred_element_type=F32))
        return 0

    lax.fori_loop(0, 4, pull_columns, 0)
    copies[2].wait()
    for q in range(blocks):
        for k in range(reads):
            column = pl.multiple_of(pattern[k, q] * BLK, BLK)
            gain_weights[q * BLK : (q + 1) * BLK, pl.ds(column, BLK)] = gain[q, k]
    for copy in copies[3:]:
        copy.wait()
    for q in range(blocks):
        lhs[:, q * BLK : (q + 1) * BLK] = lhs[:, q * BLK : (q + 1) * BLK] * mask[:, q : q + 1].astype(BF16)
    hidden = jax.nn.gelu(jnp.dot(rows_in[...], enc_in[...], preferred_element_type=F32)).astype(BF16)

    def drive_columns(at, _):
        window = pl.ds(pl.multiple_of(at * 2 * BLK, 2 * BLK), 2 * BLK)
        total = jnp.dot(lhs[...], gain_weights[:, window], preferred_element_type=F32)
        total += jnp.dot(hidden, enc_out[:, window], preferred_element_type=F32)
        split(0, at, total)
        return 0

    lax.fori_loop(0, 4, drive_columns, 0)


def merge_kernel(place, keep, came, parcel, own):
    for at in range(parcel.shape[0]):
        parcel[at] = (keep[at] + came[at].astype(F32)).astype(BF16)
    own[...] = keep[place[0]] + came[place[0]].astype(F32)


def rows_of(b, u, steps):
    return pl.ds(b * steps + u, SEG, stride=steps // SEG)


def turn(x, by, fill, backward):
    row = lax.broadcasted_iota(jnp.int32, x.shape, 0)
    if backward:
        return jnp.where(row < SEG - by, pltpu.roll(x, SEG - by, 0), fill)
    return jnp.where(row >= by, pltpu.roll(x, by, 0), fill)


def chain(factor, value, backward):
    for by in (1, 2, 4):
        value = factor * turn(value, by, 0.0, backward) + value
        factor = factor * turn(factor, by, 1.0, backward)
    return factor, value, turn(factor, 1, 1.0, backward), turn(value, 1, 0.0, backward)


def decay_kernel(traces, steps, retain, smooth, keep_r, keep_s, root, ahead_p, filt_p, rise_p, fall_p, seg_r, seg_s):
    for b in range(traces):
        span = slice(b * steps, (b + 1) * steps)
        keep_r[span, :] = retain[pl.ds(b, BLK, stride=traces), :].T
        keep_s[span, :] = smooth[pl.ds(b, BLK, stride=traces), :].T
    root[...] = jnp.sqrt(1.0 - keep_r[...] * keep_r[...])
    ones = jnp.ones((SEG, BLK), F32)
    for b in range(traces):
        filt, rise = ones, ones
        for u in range(steps // SEG):
            at = rows_of(b, u, steps)
            r, s = keep_r[at, :], keep_s[at, :]
            filt = filt * r
            filt_p[at, :] = filt
            rise_p[at, :] = rise
            rise = rise * s
        seg_r[b] = filt
        seg_s[b] = rise
        ahead, fall = ones, ones
        for u in reversed(range(steps // SEG)):
            at = rows_of(b, u, steps)
            r, s = keep_r[at, :], keep_s[at, :]
            ahead = ahead * s
            ahead_p[at, :] = ahead
            fall_p[at, :] = fall
            fall = fall * r


def scan_kernel(
    traces, steps, place,
    own, came, keep_r, keep_s, root, seg_r, seg_s,
    states, grads, before, parcel,
    source, pull, ends,
):
    others = [lax.rem(place[0] + k, 4) for k in (1, 2, 3)]
    source[...] = root[...] * (own[0] + sum(came[other, 0].astype(F32) for other in others))
    pull[...] = own[1] + sum(came[other, 1].astype(F32) for other in others)
    for b in range(traces):
        filt = jnp.zeros((SEG, BLK), F32)
        rise, ahead, fall = filt, filt, filt
        for u in range(steps // SEG):
            at = rows_of(b, u, steps)
            r, s, g, p = keep_r[at, :], keep_s[at, :], source[at, :], pull[at, :]
            filt = r * filt + g
            states[at, :] = filt
            carried = rise + p
            grads[at, :] = carried
            rise = s * carried
        for u in reversed(range(steps // SEG)):
            at = rows_of(b, u, steps)
            r, s, g, p = keep_r[at, :], keep_s[at, :], source[at, :], pull[at, :]
            later = s * ahead
            states[at, :] = states[at, :] + later
            ahead = later + g
            grads[at, :] = grads[at, :] + fall
            fall = r * (fall + p)
        for which, (factor, value, backward) in enumerate(
            ((seg_r[b], filt, False), (seg_s[b], rise, False), (seg_s[b], ahead, True), (seg_r[b], fall, True))
        ):
            whole, total, factor_before, value_before = chain(factor, value, backward)
            before[which, b, 0] = factor_before
            before[which, b, 1] = value_before
            end = 0 if backward else SEG - 1
            half, row = which // 2, (which % 2) * traces + b
            ends[half, 0, row : row + 1, :] = total[end : end + 1, :]
            ends[half, 1, row : row + 1, :] = whole[end : end + 1, :]
    me = place[2]
    for target in range(parcel.shape[0]):
        onward = target > me
        parcel[target, :SEG] = jnp.where(onward, ends[0, 0], ends[1, 0])
        parcel[target, SEG:] = jnp.where(onward, ends[0, 1], ends[1, 1])


def settle_kernel(
    traces, steps, place,
    parcel, before, states, grads, root, ahead_p, filt_p, rise_p, fall_p,
    states_bf, grads_bf,
    sums, carry,
):
    me, length = place[2], parcel.shape[0]
    onward = jnp.zeros((SEG, BLK), F32)
    back = onward
    for j in range(length):
        onward = jnp.where(j < me, parcel[j, SEG:] * onward + parcel[j, :SEG], onward)
        i = length - 1 - j
        back = jnp.where(i > me, parcel[i, SEG:] * back + parcel[i, :SEG], back)
    carry[0] = onward
    carry[1] = back
    for b in range(traces):
        filt, rise, ahead, fall = (
            before[w, b, 1] + before[w, b, 0] * carry[w // 2, (w % 2) * traces + b : (w % 2) * traces + b + 1, :]
            for w in range(4)
        )
        for u in range(steps // SEG):
            at = rows_of(b, u, steps)
            sums[0, at, :] = states[at, :] + filt_p[at, :] * filt + ahead_p[at, :] * ahead
            sums[1, at, :] = root[at, :] * (grads[at, :] + rise_p[at, :] * rise + fall_p[at, :] * fall)
    states_bf[...] = sums[0].astype(BF16)
    grads_bf[...] = sums[1].astype(BF16)


def project_kernel(dims, masked, place, *refs):
    *pieces, weights, mask, out, lhs, stage, sems = refs
    x, core = place[0], place[1]
    for k in range(4):
        column = 2 * lax.rem(x - k + 4, 4)
        for side in range(2):
            block = column + (core if side == 0 else 1 - core)
            lhs[:, pl.ds(pl.multiple_of(block * BLK, BLK), BLK)] = pieces[side * 4 + k][...]
    copies = []
    for at in range(4):
        window = slice(at * 2 * BLK, (at + 1) * 2 * BLK)
        chosen = weights[window, :] if dims is NT else weights[:, window]
        total = lax.dot_general(lhs[...], chosen, dims, preferred_element_type=F32)
        for half in range(2):
            q = 2 * at + half
            piece = total[:, half * BLK : (half + 1) * BLK]
            if masked:
                piece = piece * mask[:, q : q + 1]
            stage[:, q * BLK : (q + 1) * BLK] = piece.astype(BF16)
        copies.append(pltpu.make_async_copy(stage.at[:, window], out.at[:, window], sems.at[at]))
        copies[-1].start()
    for copy in copies:
        copy.wait()


def local(inputs, encoder_in, encoder_out, readings, available, pattern, gain, load, retain, smooth, cotangent):
    traces, steps, features = inputs.shape
    rows = traces * steps
    sensors, blocks = readings.shape[2], available.shape[2]
    states = encoder_out.shape[1]
    axis, times = lax.axis_size("state"), lax.axis_size("tm")
    at = lax.axis_index("state")
    place = jnp.stack([at // 2, at % 2, lax.axis_index("tm")]).astype(jnp.int32)
    swap = [(i, i ^ 1) for i in range(axis)]
    shift = {k: [(i, (i + 2 * k) % axis) for i in range(axis)] for k in (1, 2, 3)}
    columns = [[2 * x + core for x in range(axis // 2)] for core in range(2)]
    work = 2 * rows * sensors * states

    far = (
        load, cotangent.reshape(rows, sensors), gain, readings.reshape(rows, sensors),
        inputs.reshape(rows, features), encoder_in, encoder_out,
    )
    load_weights, gain_weights, keep, send, mask = call(
        front_kernel,
        (
            struct((states, sensors), BF16),
            struct((sensors, states), BF16),
            struct((axis // 2, 2, rows, BLK), F32),
            struct((axis // 2, 2, rows, BLK), BF16),
            struct((rows, blocks), F32),
        ),
        (place, pattern.T, available.transpose(0, 2, 1), *far),
        scratch=[pltpu.VMEM(a.shape, a.dtype) for a in far] + [pltpu.SemaphoreType.DMA((len(far),))],
        smem=2,
        hbm=len(far),
        flops=2 * work,
    )
    came = lax.ppermute(send, "state", swap)
    full, segments = struct((rows, BLK), F32), struct((traces, SEG, BLK), F32)
    keep_r, keep_s, root, ahead_p, filt_p, rise_p, fall_p, seg_r, seg_s = call(
        functools.partial(decay_kernel, traces, steps),
        (full,) * 7 + (segments,) * 2,
        (retain.reshape(-1, steps), smooth.reshape(-1, steps)),
    )
    decays = (keep_r, keep_s, root, ahead_p, filt_p, rise_p, fall_p, seg_r, seg_s)
    keep, decays = lax.optimization_barrier((keep, decays))
    keep_r, keep_s, root, ahead_p, filt_p, rise_p, fall_p, seg_r, seg_s = decays
    sums, own = call(
        merge_kernel,
        (struct(send.shape, BF16), struct((2, rows, BLK), F32)),
        (place, keep, came),
        smem=1,
    )
    sums = lax.all_to_all(sums, "state", 0, 0, axis_index_groups=columns)
    scanned, pulled, before, parcel = call(
        functools.partial(scan_kernel, traces, steps),
        (full, full, struct((4, traces, 2, SEG, BLK), F32), struct((times, 2 * SEG, BLK), F32)),
        (place, own, sums, keep_r, keep_s, root, seg_r, seg_s),
        scratch=[pltpu.VMEM((rows, BLK), F32)] * 2 + [pltpu.VMEM((2, 2, SEG, BLK), F32)],
        smem=1,
    )
    parcel = lax.all_to_all(parcel, "tm", 0, 0)
    half = struct((rows, BLK), BF16)
    states_bf, grads_bf = call(
        functools.partial(settle_kernel, traces, steps),
        (half, half),
        (place, parcel, before, scanned, pulled, root, ahead_p, filt_p, rise_p, fall_p),
        scratch=[pltpu.VMEM((2, rows, BLK), F32), pltpu.VMEM((2, SEG, BLK), F32)],
        smem=1,
    )

    def across(piece):
        return [piece] + [lax.ppermute(piece, "state", shift[k]) for k in (1, 2, 3)]

    def project(dims, masked, same, weights):
        other = [lax.ppermute(one, "state", swap) for one in same]
        (out,) = call(
            functools.partial(project_kernel, dims, masked),
            (struct((rows, sensors), BF16),),
            (place, *same, *other, weights, mask),
            scratch=[pltpu.VMEM((rows, states), BF16), pltpu.VMEM((rows, sensors), BF16), pltpu.SemaphoreType.DMA((4,))],
            smem=1,
            hbm_out=True,
            flops=work,
        )
        return out

    all_states, all_grads = across(states_bf), across(grads_bf)
    predicted = project(NN, False, all_states, load_weights)
    predicted, all_grads = lax.optimization_barrier((predicted, all_grads))
    sensor_grad = project(NT, True, all_grads, gain_weights)
    return predicted.reshape(readings.shape), sensor_grad.reshape(readings.shape)


def solution(mesh):
    placed = (
        P(None, "tm", None),
        P(None, "state"),
        P("state", None),
        P(None, "tm", "state"),
        P(None, "tm", "state"),
        P("state", None),
        P("state", None, None, None),
        P("state", None, None, None),
        P("state", None, "tm"),
        P("state", None, "tm"),
        P(None, "tm", "state"),
    )
    return jax.shard_map(
        local,
        mesh=mesh,
        in_specs=placed,
        out_specs=(P(None, "tm", "state"), P(None, "tm", "state")),
        check_vma=False,
    )
```

```python
import functools

import jax
import jax.numpy as jnp
from jax import lax
from jax.experimental import pallas as pl
from jax.experimental.pallas import tpu as pltpu
from jax.sharding import PartitionSpec as P


F32, BF16 = jnp.float32, jnp.bfloat16
VMEM = 20 << 20
BLK = 128
SEG = 8
NT = (((1,), (1,)), ((), ()))
NN = (((1,), (0,)), ((), ()))


def call(kernel, outs, operands, scratch=(), smem=0, hbm=0, hbm_out=False, flops=0):
    vmem, scalar = pl.BlockSpec(memory_space=pltpu.VMEM), pl.BlockSpec(memory_space=pltpu.SMEM)
    far = pl.BlockSpec(memory_space=pltpu.HBM)
    moved = sum(a.size * a.dtype.itemsize for a in (*operands, *outs))
    return pl.pallas_call(
        kernel,
        out_shape=outs,
        in_specs=[scalar] * smem + [vmem] * (len(operands) - smem - hbm) + [far] * hbm,
        out_specs=tuple([far if hbm_out else vmem] * len(outs)),
        scratch_shapes=list(scratch),
        compiler_params=pltpu.CompilerParams(vmem_limit_bytes=VMEM),
        cost_estimate=pl.CostEstimate(flops=flops, bytes_accessed=moved, transcendentals=0),
    )(*operands[: len(operands) - hbm], *[in_hbm(a) for a in operands[len(operands) - hbm :]])


def in_hbm(array):
    return pltpu.with_memory_space_constraint(array, pltpu.HBM)


def struct(shape, dtype):
    return jax.ShapeDtypeStruct(shape, dtype)


def front_kernel(
    place, pattern, load_far, cot_far, gain_far, available_far, readings_far, rows_far, enc_in_far, enc_out_far,
    load_weights, gain_weights, keep, send, mask,
    load, cotangent, gain, available, lhs, rows_in, enc_in, enc_out, sems,
):
    core = place[1]
    pairs = (
        (load_far, load), (cot_far, cotangent), (gain_far, gain), (available_far, available),
        (readings_far, lhs), (rows_far, rows_in), (enc_in_far, enc_in), (enc_out_far, enc_out),
    )
    copies = [pltpu.make_async_copy(far, near, sems.at[i]) for i, (far, near) in enumerate(pairs)]
    for copy in copies:
        copy.start()
    load_weights[...] = jnp.zeros_like(load_weights)
    gain_weights[...] = jnp.zeros_like(gain_weights)
    traces, blocks, steps = available.shape
    reads = pattern.shape[0]

    def split(which, at, total):
        low, high = total[:, :BLK], total[:, BLK:]
        keep[at, which] = jnp.where(core == 0, low, high)
        send[at, which] = jnp.where(core == 0, high, low).astype(BF16)

    copies[0].wait()
    for q in range(blocks):
        for k in range(reads):
            row = pl.multiple_of(pattern[k, q] * BLK, BLK)
            load_weights[pl.ds(row, BLK), q * BLK : (q + 1) * BLK] = load[q, k]
    copies[1].wait()

    def pull_columns(at, _):
        window = pl.ds(pl.multiple_of(at * 2 * BLK, 2 * BLK), 2 * BLK)
        split(1, at, lax.dot_general(cotangent[...], load_weights[window, :], NT, preferred_element_type=F32))
        return 0

    lax.fori_loop(0, 4, pull_columns, 0)
    copies[2].wait()
    for q in range(blocks):
        for k in range(reads):
            column = pl.multiple_of(pattern[k, q] * BLK, BLK)
            gain_weights[q * BLK : (q + 1) * BLK, pl.ds(column, BLK)] = gain[q, k]
    for copy in copies[3:]:
        copy.wait()
    for b in range(traces):
        mask[b * steps : (b + 1) * steps, :] = available[b].astype(F32).T
    for q in range(blocks):
        lhs[:, q * BLK : (q + 1) * BLK] = lhs[:, q * BLK : (q + 1) * BLK] * mask[:, q : q + 1].astype(BF16)
    hidden = jax.nn.gelu(jnp.dot(rows_in[...], enc_in[...], preferred_element_type=F32)).astype(BF16)

    def drive_columns(at, _):
        window = pl.ds(pl.multiple_of(at * 2 * BLK, 2 * BLK), 2 * BLK)
        total = jnp.dot(lhs[...], gain_weights[:, window], preferred_element_type=F32)
        total += jnp.dot(hidden, enc_out[:, window], preferred_element_type=F32)
        split(0, at, total)
        return 0

    lax.fori_loop(0, 4, drive_columns, 0)


def merge_kernel(place, keep, came, own, *pieces):
    own[...] = keep[place[0]] + came[place[0]].astype(F32)
    for k, piece in enumerate(pieces):
        at = lax.rem(place[0] + k + 1, keep.shape[0])
        piece[...] = (keep[at] + came[at].astype(F32)).astype(BF16)


def rows_of(b, u, steps):
    return pl.ds(b * steps + u, SEG, stride=steps // SEG)


def turn(x, by, fill, backward):
    row = lax.broadcasted_iota(jnp.int32, x.shape, 0)
    if backward:
        return jnp.where(row < SEG - by, pltpu.roll(x, SEG - by, 0), fill)
    return jnp.where(row >= by, pltpu.roll(x, by, 0), fill)


def chain(factor, value, backward):
    for by in (1, 2, 4):
        value = factor * turn(value, by, 0.0, backward) + value
        factor = factor * turn(factor, by, 1.0, backward)
    return factor, value, turn(factor, 1, 1.0, backward), turn(value, 1, 0.0, backward)


def decay_kernel(traces, steps, retain, smooth, keep_r, keep_s, root, ahead_p, filt_p, rise_p, fall_p, seg_r, seg_s):
    for b in range(traces):
        span = slice(b * steps, (b + 1) * steps)
        keep_r[span, :] = retain[pl.ds(b, BLK, stride=traces), :].T
        keep_s[span, :] = smooth[pl.ds(b, BLK, stride=traces), :].T
    root[...] = jnp.sqrt(1.0 - keep_r[...] * keep_r[...])
    ones = jnp.ones((SEG, BLK), F32)
    for b in range(traces):
        filt, rise = ones, ones
        for u in range(steps // SEG):
            at = rows_of(b, u, steps)
            r, s = keep_r[at, :], keep_s[at, :]
            filt = filt * r
            filt_p[at, :] = filt
            rise_p[at, :] = rise
            rise = rise * s
        seg_r[b] = filt
        seg_s[b] = rise
        ahead, fall = ones, ones
        for u in reversed(range(steps // SEG)):
            at = rows_of(b, u, steps)
            r, s = keep_r[at, :], keep_s[at, :]
            ahead = ahead * s
            ahead_p[at, :] = ahead
            fall_p[at, :] = fall
            fall = fall * r


def scan_kernel(
    traces, steps, place,
    own, one, two, three, keep_r, keep_s, root, seg_r, seg_s,
    states, grads, before, parcel,
    source, pull, ends,
):
    pieces = (one, two, three)
    source[...] = root[...] * (own[0] + sum(piece[0].astype(F32) for piece in pieces))
    pull[...] = own[1] + sum(piece[1].astype(F32) for piece in pieces)
    for b in range(traces):
        filt = jnp.zeros((SEG, BLK), F32)
        rise, ahead, fall = filt, filt, filt
        for u in range(steps // SEG):
            at = rows_of(b, u, steps)
            r, s, g, p = keep_r[at, :], keep_s[at, :], source[at, :], pull[at, :]
            filt = r * filt + g
            states[at, :] = filt
            carried = rise + p
            grads[at, :] = carried
            rise = s * carried
        for u in reversed(range(steps // SEG)):
            at = rows_of(b, u, steps)
            r, s, g, p = keep_r[at, :], keep_s[at, :], source[at, :], pull[at, :]
            later = s * ahead
            states[at, :] = states[at, :] + later
            ahead = later + g
            grads[at, :] = grads[at, :] + fall
            fall = r * (fall + p)
        for which, (factor, value, backward) in enumerate(
            ((seg_r[b], filt, False), (seg_s[b], rise, False), (seg_s[b], ahead, True), (seg_r[b], fall, True))
        ):
            whole, total, factor_before, value_before = chain(factor, value, backward)
            before[which, b, 0] = factor_before
            before[which, b, 1] = value_before
            end = 0 if backward else SEG - 1
            half, row = which // 2, (which % 2) * traces + b
            ends[half, 0, row : row + 1, :] = total[end : end + 1, :]
            ends[half, 1, row : row + 1, :] = whole[end : end + 1, :]
    me = place[2]
    for target in range(parcel.shape[0]):
        onward = target > me
        parcel[target, :SEG] = jnp.where(onward, ends[0, 0], ends[1, 0])
        parcel[target, SEG:] = jnp.where(onward, ends[0, 1], ends[1, 1])


def settle_kernel(
    traces, steps, place,
    parcel, before, states, grads, root, ahead_p, filt_p, rise_p, fall_p,
    smoothed,
    sums, carry,
):
    me, length = place[2], parcel.shape[0]
    onward = jnp.zeros((SEG, BLK), F32)
    back = onward
    for j in range(length):
        onward = jnp.where(j < me, parcel[j, SEG:] * onward + parcel[j, :SEG], onward)
        i = length - 1 - j
        back = jnp.where(i > me, parcel[i, SEG:] * back + parcel[i, :SEG], back)
    carry[0] = onward
    carry[1] = back
    for b in range(traces):
        filt, rise, ahead, fall = (
            before[w, b, 1] + before[w, b, 0] * carry[w // 2, (w % 2) * traces + b : (w % 2) * traces + b + 1, :]
            for w in range(4)
        )
        for u in range(steps // SEG):
            at = rows_of(b, u, steps)
            sums[0, at, :] = states[at, :] + filt_p[at, :] * filt + ahead_p[at, :] * ahead
            sums[1, at, :] = root[at, :] * (grads[at, :] + rise_p[at, :] * rise + fall_p[at, :] * fall)
    smoothed[...] = sums[...].astype(BF16)


def project_kernel(shift, last, place, mine, partner, load_weights, gain_weights, mask, *refs):
    before, refs = ((), refs) if shift == 0 else (refs[:2], refs[2:])
    outs, lhs, *rest = refs[:2], *refs[2:]
    core = place[1]
    block = pl.multiple_of(2 * BLK * lax.rem(place[0] - shift + 4, 4), 2 * BLK)
    states = pl.ds(block, 2 * BLK)
    copies = []
    for which in range(2):
        for side, piece in enumerate((mine, partner)):
            column = pl.multiple_of(BLK * (core if side == 0 else 1 - core), BLK)
            lhs[which, :, pl.ds(column, BLK)] = piece[which]
        for at in range(4):
            window = slice(at * 2 * BLK, (at + 1) * 2 * BLK)
            if which == 0:
                total = lax.dot_general(lhs[0], load_weights[states, window], NN, preferred_element_type=F32)
            else:
                total = lax.dot_general(lhs[1], gain_weights[window, states], NT, preferred_element_type=F32)
            if before:
                total = before[which][:, window] + total
            if not last:
                outs[which][:, window] = total
                continue
            stage, sems = rest
            for half in range(2):
                q = 2 * at + half
                piece = total[:, half * BLK : (half + 1) * BLK]
                if which == 1:
                    piece = piece * mask[:, q : q + 1]
                stage[which, :, q * BLK : (q + 1) * BLK] = piece.astype(BF16)
            copies.append(
                pltpu.make_async_copy(stage.at[which, :, window], outs[which].at[:, window], sems.at[which, at])
            )
            copies[-1].start()
    for copy in copies:
        copy.wait()


def local(inputs, encoder_in, encoder_out, readings, available, pattern, gain, load, retain, smooth, cotangent):
    traces, steps, features = inputs.shape
    rows = traces * steps
    sensors, blocks = readings.shape[2], available.shape[2]
    states = encoder_out.shape[1]
    axis, times = lax.axis_size("state"), lax.axis_size("tm")
    at = lax.axis_index("state")
    place = jnp.stack([at // 2, at % 2, lax.axis_index("tm")]).astype(jnp.int32)
    swap = [(i, i ^ 1) for i in range(axis)]

    def across(pieces):
        moved = {k: lax.ppermute(pieces[k - 1], "state", [(i, (i + 2 * k) % axis) for i in range(axis)]) for k in (1, 3, 2)}
        return [moved[k] for k in (1, 2, 3)]

    work = 2 * rows * sensors * states

    far = (
        load, cotangent.reshape(rows, sensors), gain, available.transpose(0, 2, 1),
        readings.reshape(rows, sensors), inputs.reshape(rows, features), encoder_in, encoder_out,
    )
    load_weights, gain_weights, keep, send, mask = call(
        front_kernel,
        (
            struct((states, sensors), BF16),
            struct((sensors, states), BF16),
            struct((axis // 2, 2, rows, BLK), F32),
            struct((axis // 2, 2, rows, BLK), BF16),
            struct((rows, blocks), F32),
        ),
        (place, in_hbm(pattern.T), *far),
        scratch=[pltpu.VMEM(a.shape, a.dtype) for a in far] + [pltpu.SemaphoreType.DMA((len(far),))],
        smem=2,
        hbm=len(far),
        flops=2 * work,
    )
    came = lax.ppermute(send, "state", swap)
    full, segments = struct((rows, BLK), F32), struct((traces, SEG, BLK), F32)
    keep_r, keep_s, root, ahead_p, filt_p, rise_p, fall_p, seg_r, seg_s = call(
        functools.partial(decay_kernel, traces, steps),
        (full,) * 7 + (segments,) * 2,
        (retain.reshape(-1, steps), smooth.reshape(-1, steps)),
    )
    decays = (keep_r, keep_s, root, ahead_p, filt_p, rise_p, fall_p, seg_r, seg_s)
    keep, decays = lax.optimization_barrier((keep, decays))
    keep_r, keep_s, root, ahead_p, filt_p, rise_p, fall_p, seg_r, seg_s = decays
    both = struct((2, rows, BLK), BF16)
    own, *sums = call(merge_kernel, (struct(both.shape, F32),) + (both,) * 3, (place, keep, came), smem=1)
    sums = across(sums)
    scanned, pulled, before, parcel = call(
        functools.partial(scan_kernel, traces, steps),
        (full, full, struct((4, traces, 2, SEG, BLK), F32), struct((times, 2 * SEG, BLK), F32)),
        (place, own, *sums, keep_r, keep_s, root, seg_r, seg_s),
        scratch=[pltpu.VMEM((rows, BLK), F32)] * 2 + [pltpu.VMEM((2, 2, SEG, BLK), F32)],
        smem=1,
    )
    parcel = lax.all_to_all(parcel, "tm", 0, 0)
    (smoothed,) = call(
        functools.partial(settle_kernel, traces, steps),
        (both,),
        (place, parcel, before, scanned, pulled, root, ahead_p, filt_p, rise_p, fall_p),
        scratch=[pltpu.VMEM((2, rows, BLK), F32), pltpu.VMEM((2, SEG, BLK), F32)],
        smem=1,
    )
    same = [smoothed, *across([smoothed] * 3)]
    totals = ()
    for shift in (0, 1, 3, 2):
        last = shift == 2
        if shift == 1:
            totals, same[1] = lax.optimization_barrier((totals, same[1]))
            totals, same[3] = lax.optimization_barrier((totals, same[3]))
        if shift == 3:
            totals, same[2] = lax.optimization_barrier((totals, same[2]))
        partner = lax.ppermute(same[shift], "state", swap)
        totals = call(
            functools.partial(project_kernel, shift, last),
            (struct((rows, sensors), BF16 if last else F32),) * 2,
            (place, same[shift], partner, load_weights, gain_weights, mask, *totals),
            scratch=[pltpu.VMEM((2, rows, 2 * BLK), BF16)]
            + ([pltpu.VMEM((2, rows, sensors), BF16), pltpu.SemaphoreType.DMA((2, 4))] if last else []),
            smem=1,
            hbm_out=last,
            flops=work // 2,
        )
    predicted, sensor_grad = totals
    return predicted.reshape(readings.shape), sensor_grad.reshape(readings.shape)


def solution(mesh):
    placed = (
        P(None, "tm", None),
        P(None, "state"),
        P("state", None),
        P(None, "tm", "state"),
        P(None, "tm", "state"),
        P("state", None),
        P("state", None, None, None),
        P("state", None, None, None),
        P("state", None, "tm"),
        P("state", None, "tm"),
        P(None, "tm", "state"),
    )
    return jax.shard_map(
        local,
        mesh=mesh,
        in_specs=placed,
        out_specs=(P(None, "tm", "state"), P(None, "tm", "state")),
        check_vma=False,
    )
```

```python
import functools

import jax
import jax.numpy as jnp
from jax import lax
from jax.experimental import pallas as pl
from jax.experimental.pallas import tpu as pltpu
from jax.sharding import PartitionSpec as P


F32, BF16 = jnp.float32, jnp.bfloat16
VMEM = 20 << 20
BLK = 128
SEG = 8
NT = (((1,), (1,)), ((), ()))
NN = (((1,), (0,)), ((), ()))


def call(kernel, outs, operands, scratch=(), smem=0, hbm=0, hbm_out=False, flops=0):
    vmem, scalar = pl.BlockSpec(memory_space=pltpu.VMEM), pl.BlockSpec(memory_space=pltpu.SMEM)
    far = pl.BlockSpec(memory_space=pltpu.HBM)
    moved = sum(a.size * a.dtype.itemsize for a in (*operands, *outs))
    return pl.pallas_call(
        kernel,
        out_shape=outs,
        in_specs=[scalar] * smem + [vmem] * (len(operands) - smem - hbm) + [far] * hbm,
        out_specs=tuple([far if hbm_out else vmem] * len(outs)),
        scratch_shapes=list(scratch),
        compiler_params=pltpu.CompilerParams(vmem_limit_bytes=VMEM),
        cost_estimate=pl.CostEstimate(flops=flops, bytes_accessed=moved, transcendentals=0),
    )(*operands[: len(operands) - hbm], *[in_hbm(a) for a in operands[len(operands) - hbm :]])


def in_hbm(array):
    return pltpu.with_memory_space_constraint(array, pltpu.HBM)


def struct(shape, dtype):
    return jax.ShapeDtypeStruct(shape, dtype)


def split(place, keep, send, at, total):
    mine = place[1] == 0
    low, high = total[:, :BLK], total[:, BLK:]
    keep[at] = jnp.where(mine, low, high)
    send[at] = jnp.where(mine, high, low).astype(BF16)


def window_of(at):
    return slice(at * 2 * BLK, (at + 1) * 2 * BLK)


def pull_kernel(
    place, pattern, load_far, cot_far, rows_far, enc_in_far, enc_out_far, gain_far, available_far, readings_far,
    weights, keep, send, rows_in, enc_in, enc_out, gain, available, readings,
    load, cotangent, sems,
):
    pairs = (
        (load_far, load), (cot_far, cotangent), (rows_far, rows_in), (enc_in_far, enc_in), (enc_out_far, enc_out),
        (gain_far, gain), (available_far, available), (readings_far, readings),
    )
    copies = [pltpu.make_async_copy(far, near, sems.at[i]) for i, (far, near) in enumerate(pairs)]
    for copy in copies:
        copy.start()
    weights[...] = jnp.zeros_like(weights)
    copies[0].wait()
    for q in range(load.shape[0]):
        for k in range(load.shape[1]):
            row = pl.multiple_of(pattern[k, q] * BLK, BLK)
            weights[pl.ds(row, BLK), q * BLK : (q + 1) * BLK] = load[q, k]
    copies[1].wait()
    for at in range(keep.shape[0]):
        total = lax.dot_general(cotangent[...], weights[window_of(at), :], NT, preferred_element_type=F32)
        split(place, keep, send, at, total)
    for copy in copies[2:]:
        copy.wait()


def drive_kernel(
    place, pattern, rows_in, enc_in, enc_out, gain, available, readings,
    weights, keep, send, mask,
    lhs,
):
    traces, blocks, steps = available.shape
    hidden = jax.nn.gelu(jnp.dot(rows_in[...], enc_in[...], preferred_element_type=F32)).astype(BF16)
    weights[...] = jnp.zeros_like(weights)
    for b in range(traces):
        mask[b * steps : (b + 1) * steps, :] = available[b].astype(F32).T
    for q in range(blocks):
        for k in range(gain.shape[1]):
            column = pl.multiple_of(pattern[k, q] * BLK, BLK)
            weights[q * BLK : (q + 1) * BLK, pl.ds(column, BLK)] = gain[q, k]
        lhs[:, q * BLK : (q + 1) * BLK] = readings[:, q * BLK : (q + 1) * BLK] * mask[:, q : q + 1].astype(BF16)
    for at in range(keep.shape[0]):
        total = jnp.dot(lhs[...], weights[:, window_of(at)], preferred_element_type=F32)
        total += jnp.dot(hidden, enc_out[:, window_of(at)], preferred_element_type=F32)
        split(place, keep, send, at, total)


def merge_kernel(shift, place, keep_a, keep_b, came_a, came_b, piece):
    at = lax.rem(place[0] + shift, keep_a.shape[0])
    for which, (keep, came) in enumerate(((keep_a, came_a), (keep_b, came_b))):
        piece[which] = (keep[at] + came[at].astype(F32)).astype(piece.dtype)


def rows_of(b, u, steps):
    return pl.ds(b * steps + u, SEG, stride=steps // SEG)


def turn(x, by, fill, backward):
    row = lax.broadcasted_iota(jnp.int32, x.shape, 0)
    if backward:
        return jnp.where(row < SEG - by, pltpu.roll(x, SEG - by, 0), fill)
    return jnp.where(row >= by, pltpu.roll(x, by, 0), fill)


def chain(factor, value, backward):
    for by in (1, 2, 4):
        value = factor * turn(value, by, 0.0, backward) + value
        factor = factor * turn(factor, by, 1.0, backward)
    return factor, value, turn(factor, 1, 1.0, backward), turn(value, 1, 0.0, backward)


def decay_kernel(traces, steps, retain, smooth, keep_r, keep_s, root, ahead_p, filt_p, rise_p, fall_p, seg_r, seg_s):
    for b in range(traces):
        span = slice(b * steps, (b + 1) * steps)
        keep_r[span, :] = retain[pl.ds(b, BLK, stride=traces), :].T
        keep_s[span, :] = smooth[pl.ds(b, BLK, stride=traces), :].T
    root[...] = jnp.sqrt(1.0 - keep_r[...] * keep_r[...])
    ones = jnp.ones((SEG, BLK), F32)
    for b in range(traces):
        filt, rise = ones, ones
        for u in range(steps // SEG):
            at = rows_of(b, u, steps)
            r, s = keep_r[at, :], keep_s[at, :]
            filt = filt * r
            filt_p[at, :] = filt
            rise_p[at, :] = rise
            rise = rise * s
        seg_r[b] = filt
        seg_s[b] = rise
        ahead, fall = ones, ones
        for u in reversed(range(steps // SEG)):
            at = rows_of(b, u, steps)
            r, s = keep_r[at, :], keep_s[at, :]
            ahead = ahead * s
            ahead_p[at, :] = ahead
            fall_p[at, :] = fall
            fall = fall * r


def scan_kernel(
    traces, steps, place,
    own, one, two, three, keep_r, keep_s, root, seg_r, seg_s,
    states, grads, before, parcel,
    source, pull, ends,
):
    pieces = (one, two, three)
    source[...] = root[...] * (own[0] + sum(piece[0].astype(F32) for piece in pieces))
    pull[...] = own[1] + sum(piece[1].astype(F32) for piece in pieces)
    for b in range(traces):
        filt = jnp.zeros((SEG, BLK), F32)
        rise, ahead, fall = filt, filt, filt
        for u in range(steps // SEG):
            at = rows_of(b, u, steps)
            r, s, g, p = keep_r[at, :], keep_s[at, :], source[at, :], pull[at, :]
            filt = r * filt + g
            states[at, :] = filt
            carried = rise + p
            grads[at, :] = carried
            rise = s * carried
        for u in reversed(range(steps // SEG)):
            at = rows_of(b, u, steps)
            r, s, g, p = keep_r[at, :], keep_s[at, :], source[at, :], pull[at, :]
            later = s * ahead
            states[at, :] = states[at, :] + later
            ahead = later + g
            grads[at, :] = grads[at, :] + fall
            fall = r * (fall + p)
        for which, (factor, value, backward) in enumerate(
            ((seg_r[b], filt, False), (seg_s[b], rise, False), (seg_s[b], ahead, True), (seg_r[b], fall, True))
        ):
            whole, total, factor_before, value_before = chain(factor, value, backward)
            before[which, b, 0] = factor_before
            before[which, b, 1] = value_before
            end = 0 if backward else SEG - 1
            half, row = which // 2, (which % 2) * traces + b
            ends[half, 0, row : row + 1, :] = total[end : end + 1, :]
            ends[half, 1, row : row + 1, :] = whole[end : end + 1, :]
    me = place[2]
    for target in range(parcel.shape[0]):
        onward = target > me
        parcel[target, :SEG] = jnp.where(onward, ends[0, 0], ends[1, 0])
        parcel[target, SEG:] = jnp.where(onward, ends[0, 1], ends[1, 1])


def settle_kernel(
    traces, steps, place,
    parcel, before, states, grads, root, ahead_p, filt_p, rise_p, fall_p,
    smoothed, states_bf, grads_bf,
    sums, carry,
):
    me, length = place[2], parcel.shape[0]
    onward = jnp.zeros((SEG, BLK), F32)
    back = onward
    for j in range(length):
        onward = jnp.where(j < me, parcel[j, SEG:] * onward + parcel[j, :SEG], onward)
        i = length - 1 - j
        back = jnp.where(i > me, parcel[i, SEG:] * back + parcel[i, :SEG], back)
    carry[0] = onward
    carry[1] = back
    for b in range(traces):
        filt, rise, ahead, fall = (
            before[w, b, 1] + before[w, b, 0] * carry[w // 2, (w % 2) * traces + b : (w % 2) * traces + b + 1, :]
            for w in range(4)
        )
        for u in range(steps // SEG):
            at = rows_of(b, u, steps)
            sums[0, at, :] = states[at, :] + filt_p[at, :] * filt + ahead_p[at, :] * ahead
            sums[1, at, :] = root[at, :] * (grads[at, :] + rise_p[at, :] * rise + fall_p[at, :] * fall)
    smoothed[...] = sums[...].astype(BF16)
    states_bf[0] = sums[0].astype(BF16)
    grads_bf[0] = sums[1].astype(BF16)


def project_kernel(shift, chains, last, place, load_weights, gain_weights, mask, *refs):
    count = len(chains)
    mine, partner = refs[:2]
    refs = refs[2:]
    before = ()
    if shift:
        before, refs = refs[:count], refs[count:]
    outs, lhs, rest = refs[:count], refs[count], refs[count + 1 :]
    core = place[1]
    block = pl.multiple_of(2 * BLK * lax.rem(place[0] - shift + 4, 4), 2 * BLK)
    states = pl.ds(block, 2 * BLK)
    copies = []
    for i, chain_id in enumerate(chains):
        for side, piece in enumerate((mine, partner)):
            column = pl.multiple_of(BLK * (core if side == 0 else 1 - core), BLK)
            lhs[i, :, pl.ds(column, BLK)] = piece[i]
        for at in range(4):
            window = window_of(at)
            if chain_id == 0:
                total = lax.dot_general(lhs[i], load_weights[states, window], NN, preferred_element_type=F32)
            else:
                total = lax.dot_general(lhs[i], gain_weights[window, states], NT, preferred_element_type=F32)
            if before:
                total = before[i][:, window] + total
            if not last:
                outs[i][:, window] = total
                continue
            stage, sems = rest
            for half in range(2):
                q = 2 * at + half
                part = total[:, half * BLK : (half + 1) * BLK]
                if chain_id == 1:
                    part = part * mask[:, q : q + 1]
                stage[i, :, q * BLK : (q + 1) * BLK] = part.astype(BF16)
            copies.append(pltpu.make_async_copy(stage.at[i, :, window], outs[i].at[:, window], sems.at[i, at]))
            copies[-1].start()
    for copy in copies:
        copy.wait()


def local(inputs, encoder_in, encoder_out, readings, available, pattern, gain, load, retain, smooth, cotangent):
    traces, steps, features = inputs.shape
    rows = traces * steps
    sensors, blocks = readings.shape[2], available.shape[2]
    states = encoder_out.shape[1]
    axis, times = lax.axis_size("state"), lax.axis_size("tm")
    at = lax.axis_index("state")
    place = jnp.stack([at // 2, at % 2, lax.axis_index("tm")]).astype(jnp.int32)
    swap = [(i, i ^ 1) for i in range(axis)]

    work = 2 * rows * sensors * states
    both = struct((2, rows, BLK), BF16)

    def across(piece, shift):
        return lax.ppermute(piece, "state", [(i, (i + 2 * shift) % axis) for i in range(axis)])

    near = (
        inputs.reshape(rows, features), encoder_in, encoder_out, gain, available.transpose(0, 2, 1),
        readings.reshape(rows, sensors),
    )
    pulled_from = (load, cotangent.reshape(rows, sensors))
    table = in_hbm(pattern.T)
    chips = axis // 2
    parts = (struct((chips, rows, BLK), F32), struct((chips, rows, BLK), BF16))
    load_weights, keep_b, send_b, *near = call(
        pull_kernel,
        (struct((states, sensors), BF16), *parts, *(struct(a.shape, a.dtype) for a in near)),
        (place, table, *pulled_from, *near),
        scratch=[pltpu.VMEM(a.shape, a.dtype) for a in pulled_from] + [pltpu.SemaphoreType.DMA((8,))],
        smem=2,
        hbm=8,
        flops=work,
    )
    came_b = lax.ppermute(send_b, "state", swap)
    gain_weights, keep_a, send_a, mask = call(
        drive_kernel,
        (struct((sensors, states), BF16), *parts, struct((rows, blocks), F32)),
        (place, table, *near),
        scratch=[pltpu.VMEM((rows, sensors), BF16)],
        smem=2,
        flops=work,
    )
    came_a = lax.ppermute(send_a, "state", swap)
    full, segments = struct((rows, BLK), F32), struct((traces, SEG, BLK), F32)
    keep_r, keep_s, root, ahead_p, filt_p, rise_p, fall_p, seg_r, seg_s = call(
        functools.partial(decay_kernel, traces, steps),
        (full,) * 7 + (segments,) * 2,
        (retain.reshape(-1, steps), smooth.reshape(-1, steps)),
    )
    decays = (keep_r, keep_s, root, ahead_p, filt_p, rise_p, fall_p, seg_r, seg_s)
    keep_a, decays = lax.optimization_barrier((keep_a, decays))
    keep_r, keep_s, root, ahead_p, filt_p, rise_p, fall_p, seg_r, seg_s = decays
    both = struct((2, rows, BLK), BF16)
    sums = {}
    for shift in (1, 3, 2, 0):
        (piece,) = call(
            functools.partial(merge_kernel, shift),
            (both if shift else struct(both.shape, F32),),
            (place, keep_a, keep_b, came_a, came_b),
            smem=1,
        )
        sums[shift] = across(piece, shift) if shift else piece
    own, one, two, three = (sums[k] for k in range(4))
    scanned, pulled, before, parcel = call(
        functools.partial(scan_kernel, traces, steps),
        (full, full, struct((4, traces, 2, SEG, BLK), F32), struct((times, 2 * SEG, BLK), F32)),
        (place, own, one, two, three, keep_r, keep_s, root, seg_r, seg_s),
        scratch=[pltpu.VMEM((rows, BLK), F32)] * 2 + [pltpu.VMEM((2, 2, SEG, BLK), F32)],
        smem=1,
    )
    parcel = lax.all_to_all(parcel, "tm", 0, 0)
    half = struct((1, rows, BLK), BF16)
    smoothed, states_bf, grads_bf = call(
        functools.partial(settle_kernel, traces, steps),
        (both, half, half),
        (place, parcel, before, scanned, pulled, root, ahead_p, filt_p, rise_p, fall_p),
        scratch=[pltpu.VMEM((2, rows, BLK), F32), pltpu.VMEM((2, SEG, BLK), F32)],
        smem=1,
    )
    one, three = across(smoothed, 1), across(smoothed, 3)
    far_states = across(states_bf, 2)
    far_grads = across(grads_bf, 2)

    def project(shift, chains, mine, totals):
        last = shift == 2
        partner = lax.ppermute(mine, "state", swap)
        return call(
            functools.partial(project_kernel, shift, chains, last),
            (struct((rows, sensors), BF16 if last else F32),) * len(chains),
            (place, load_weights, gain_weights, mask, mine, partner, *totals),
            scratch=[pltpu.VMEM((len(chains), rows, 2 * BLK), BF16)]
            + ([pltpu.VMEM((1, rows, sensors), BF16), pltpu.SemaphoreType.DMA((1, 4))] if last else []),
            smem=1,
            hbm_out=last,
            flops=work * len(chains) // 4,
        )

    totals = project(0, (0, 1), smoothed, ())
    totals, one = lax.optimization_barrier((totals, one))
    totals, three = lax.optimization_barrier((totals, three))
    totals = project(1, (0, 1), one, totals)
    totals, far_states = lax.optimization_barrier((totals, far_states))
    totals = project(3, (0, 1), three, totals)
    (predicted,) = project(2, (0,), far_states, totals[:1])
    predicted, far_grads = lax.optimization_barrier((predicted, far_grads))
    (sensor_grad,) = project(2, (1,), far_grads, totals[1:])
    return predicted.reshape(readings.shape), sensor_grad.reshape(readings.shape)


def solution(mesh):
    placed = (
        P(None, "tm", None),
        P(None, "state"),
        P("state", None),
        P(None, "tm", "state"),
        P(None, "tm", "state"),
        P("state", None),
        P("state", None, None, None),
        P("state", None, None, None),
        P("state", None, "tm"),
        P("state", None, "tm"),
        P(None, "tm", "state"),
    )
    return jax.shard_map(
        local,
        mesh=mesh,
        in_specs=placed,
        out_specs=(P(None, "tm", "state"), P(None, "tm", "state")),
        check_vma=False,
    )
```

```python
import functools

import jax
import jax.numpy as jnp
from jax import lax
from jax.experimental import pallas as pl
from jax.experimental.pallas import tpu as pltpu
from jax.sharding import PartitionSpec as P


F32, BF16 = jnp.float32, jnp.bfloat16
VMEM = 20 << 20
BLK = 128
SEG = 8
NT = (((1,), (1,)), ((), ()))
NN = (((1,), (0,)), ((), ()))


def call(kernel, outs, operands, scratch=(), hbm=0, hbm_out=False, flops=0):
    vmem = pl.BlockSpec(memory_space=pltpu.VMEM)
    far = pl.BlockSpec(memory_space=pltpu.HBM)
    moved = sum(a.size * a.dtype.itemsize for a in (*operands, *outs))
    return pl.pallas_call(
        kernel,
        out_shape=outs,
        in_specs=[vmem] * (len(operands) - hbm) + [far] * hbm,
        out_specs=tuple([far if hbm_out else vmem] * len(outs)),
        scratch_shapes=list(scratch),
        compiler_params=pltpu.CompilerParams(vmem_limit_bytes=VMEM),
        cost_estimate=pl.CostEstimate(flops=flops, bytes_accessed=moved, transcendentals=0),
    )(*operands[: len(operands) - hbm], *[in_hbm(a) for a in operands[len(operands) - hbm :]])


def in_hbm(array):
    return pltpu.with_memory_space_constraint(array, pltpu.HBM)


def struct(shape, dtype):
    return jax.ShapeDtypeStruct(shape, dtype)


def here():
    at = lax.axis_index("state")
    return lax.div(at, 2), lax.rem(at, 2)


def split(keep, send, at, total):
    mine = here()[1] == 0
    low, high = total[:, :BLK], total[:, BLK:]
    keep[at] = jnp.where(mine, low, high)
    send[at] = jnp.where(mine, high, low).astype(BF16)


def window_of(at):
    return slice(at * 2 * BLK, (at + 1) * 2 * BLK)


def pull_kernel(
    table_far, load_far, cot_far, rows_far, enc_in_far, enc_out_far, gain_far, available_far, readings_far,
    weights, keep, send, rows_in, enc_in, enc_out, gain, available, readings,
    pattern, load, cotangent, sems,
):
    pairs = (
        (table_far, pattern),
        (load_far, load), (cot_far, cotangent), (rows_far, rows_in), (enc_in_far, enc_in), (enc_out_far, enc_out),
        (gain_far, gain), (available_far, available), (readings_far, readings),
    )
    copies = [pltpu.make_async_copy(far, near, sems.at[i]) for i, (far, near) in enumerate(pairs)]
    for copy in copies:
        copy.start()
    weights[...] = jnp.zeros_like(weights)
    copies[0].wait()
    copies[1].wait()
    for q in range(load.shape[0]):
        for k in range(load.shape[1]):
            row = pl.multiple_of(pattern[k, q] * BLK, BLK)
            weights[pl.ds(row, BLK), q * BLK : (q + 1) * BLK] = load[q, k]
    copies[2].wait()
    for at in range(keep.shape[0]):
        total = lax.dot_general(cotangent[...], weights[window_of(at), :], NT, preferred_element_type=F32)
        split(keep, send, at, total)
    for copy in copies[3:]:
        copy.wait()


def drive_kernel(
    rows_in, enc_in, enc_out, gain, available, readings, table_far,
    weights, keep, send, mask,
    lhs, pattern, sem,
):
    fetch = pltpu.make_async_copy(table_far, pattern, sem)
    fetch.start()
    traces, blocks, steps = available.shape
    hidden = jax.nn.gelu(jnp.dot(rows_in[...], enc_in[...], preferred_element_type=F32)).astype(BF16)
    weights[...] = jnp.zeros_like(weights)
    for b in range(traces):
        mask[b * steps : (b + 1) * steps, :] = available[b].astype(F32).T
    fetch.wait()
    for q in range(blocks):
        for k in range(gain.shape[1]):
            column = pl.multiple_of(pattern[k, q] * BLK, BLK)
            weights[q * BLK : (q + 1) * BLK, pl.ds(column, BLK)] = gain[q, k]
        lhs[:, q * BLK : (q + 1) * BLK] = readings[:, q * BLK : (q + 1) * BLK] * mask[:, q : q + 1].astype(BF16)
    for at in range(keep.shape[0]):
        total = jnp.dot(lhs[...], weights[:, window_of(at)], preferred_element_type=F32)
        total += jnp.dot(hidden, enc_out[:, window_of(at)], preferred_element_type=F32)
        split(keep, send, at, total)


def merge_kernel(keep_a, keep_b, came_a, came_b, own, *pieces):
    x, _ = here()
    for which, (keep, came) in enumerate(((keep_a, came_a), (keep_b, came_b))):
        for k, piece in enumerate((own, *pieces)):
            at = lax.rem(x + k, keep.shape[0])
            piece[which] = (keep[at] + came[at].astype(F32)).astype(piece.dtype)


def rows_of(b, u, steps):
    return pl.ds(b * steps + u, SEG, stride=steps // SEG)


def turn(x, by, fill, backward):
    row = lax.broadcasted_iota(jnp.int32, x.shape, 0)
    if backward:
        return jnp.where(row < SEG - by, pltpu.roll(x, SEG - by, 0), fill)
    return jnp.where(row >= by, pltpu.roll(x, by, 0), fill)


def chain(factor, value, backward):
    for by in (1, 2, 4):
        value = factor * turn(value, by, 0.0, backward) + value
        factor = factor * turn(factor, by, 1.0, backward)
    return factor, value, turn(factor, 1, 1.0, backward), turn(value, 1, 0.0, backward)


def decay_kernel(traces, steps, retain, smooth, keep_r, keep_s, root, ahead_p, filt_p, rise_p, fall_p, seg_r, seg_s):
    for b in range(traces):
        span = slice(b * steps, (b + 1) * steps)
        keep_r[span, :] = retain[pl.ds(b, BLK, stride=traces), :].T
        keep_s[span, :] = smooth[pl.ds(b, BLK, stride=traces), :].T
    root[...] = jnp.sqrt(1.0 - keep_r[...] * keep_r[...])
    ones = jnp.ones((SEG, BLK), F32)
    for b in range(traces):
        filt, rise = ones, ones
        for u in range(steps // SEG):
            at = rows_of(b, u, steps)
            r, s = keep_r[at, :], keep_s[at, :]
            filt = filt * r
            filt_p[at, :] = filt
            rise_p[at, :] = rise
            rise = rise * s
        seg_r[b] = filt
        seg_s[b] = rise
        ahead, fall = ones, ones
        for u in reversed(range(steps // SEG)):
            at = rows_of(b, u, steps)
            r, s = keep_r[at, :], keep_s[at, :]
            ahead = ahead * s
            ahead_p[at, :] = ahead
            fall_p[at, :] = fall
            fall = fall * r


def scan_kernel(
    traces, steps,
    own, one, two, three, keep_r, keep_s, root, seg_r, seg_s,
    states, grads, before, parcel,
    source, pull, ends,
):
    pieces = (one, two, three)
    source[...] = root[...] * (own[0] + sum(piece[0].astype(F32) for piece in pieces))
    pull[...] = own[1] + sum(piece[1].astype(F32) for piece in pieces)
    for b in range(traces):
        filt = jnp.zeros((SEG, BLK), F32)
        rise, ahead, fall = filt, filt, filt
        for u in range(steps // SEG):
            at = rows_of(b, u, steps)
            r, s, g, p = keep_r[at, :], keep_s[at, :], source[at, :], pull[at, :]
            filt = r * filt + g
            states[at, :] = filt
            carried = rise + p
            grads[at, :] = carried
            rise = s * carried
        for u in reversed(range(steps // SEG)):
            at = rows_of(b, u, steps)
            r, s, g, p = keep_r[at, :], keep_s[at, :], source[at, :], pull[at, :]
            later = s * ahead
            states[at, :] = states[at, :] + later
            ahead = later + g
            grads[at, :] = grads[at, :] + fall
            fall = r * (fall + p)
        for which, (factor, value, backward) in enumerate(
            ((seg_r[b], filt, False), (seg_s[b], rise, False), (seg_s[b], ahead, True), (seg_r[b], fall, True))
        ):
            whole, total, factor_before, value_before = chain(factor, value, backward)
            before[which, b, 0] = factor_before
            before[which, b, 1] = value_before
            end = 0 if backward else SEG - 1
            half, row = which // 2, (which % 2) * traces + b
            ends[half, 0, row : row + 1, :] = total[end : end + 1, :]
            ends[half, 1, row : row + 1, :] = whole[end : end + 1, :]
    me = lax.axis_index("tm")
    for target in range(parcel.shape[0]):
        onward = target > me
        parcel[target, :SEG] = jnp.where(onward, ends[0, 0], ends[1, 0])
        parcel[target, SEG:] = jnp.where(onward, ends[0, 1], ends[1, 1])


def settle_kernel(
    traces, steps,
    parcel, before, states, grads, root, ahead_p, filt_p, rise_p, fall_p,
    smoothed,
    sums, carry,
):
    me, length = lax.axis_index("tm"), parcel.shape[0]
    onward = jnp.zeros((SEG, BLK), F32)
    back = onward
    for j in range(length):
        onward = jnp.where(j < me, parcel[j, SEG:] * onward + parcel[j, :SEG], onward)
        i = length - 1 - j
        back = jnp.where(i > me, parcel[i, SEG:] * back + parcel[i, :SEG], back)
    carry[0] = onward
    carry[1] = back
    for b in range(traces):
        filt, rise, ahead, fall = (
            before[w, b, 1] + before[w, b, 0] * carry[w // 2, (w % 2) * traces + b : (w % 2) * traces + b + 1, :]
            for w in range(4)
        )
        for u in range(steps // SEG):
            at = rows_of(b, u, steps)
            sums[0, at, :] = states[at, :] + filt_p[at, :] * filt + ahead_p[at, :] * ahead
            sums[1, at, :] = root[at, :] * (grads[at, :] + rise_p[at, :] * rise + fall_p[at, :] * fall)
    smoothed[...] = sums[...].astype(BF16)


def project_kernel(shift, last, mine, partner, load_weights, gain_weights, mask, *refs):
    before, refs = ((), refs) if shift == 0 else (refs[:2], refs[2:])
    outs, lhs, *rest = refs[:2], *refs[2:]
    x, core = here()
    block = pl.multiple_of(2 * BLK * lax.rem(x - shift + 4, 4), 2 * BLK)
    states = pl.ds(block, 2 * BLK)
    copies = []
    for which in range(2):
        for side, piece in enumerate((mine, partner)):
            column = pl.multiple_of(BLK * (core if side == 0 else 1 - core), BLK)
            lhs[which, :, pl.ds(column, BLK)] = piece[which]
        for at in range(4):
            window = slice(at * 2 * BLK, (at + 1) * 2 * BLK)
            if which == 0:
                total = lax.dot_general(lhs[0], load_weights[states, window], NN, preferred_element_type=F32)
            else:
                total = lax.dot_general(lhs[1], gain_weights[window, states], NT, preferred_element_type=F32)
            if before:
                total = before[which][:, window] + total
            if not last:
                outs[which][:, window] = total
                continue
            stage, sems = rest
            for half in range(2):
                q = 2 * at + half
                piece = total[:, half * BLK : (half + 1) * BLK]
                if which == 1:
                    piece = piece * mask[:, q : q + 1]
                stage[which, :, q * BLK : (q + 1) * BLK] = piece.astype(BF16)
            if at % 2:
                window = slice((at - 1) * 2 * BLK, (at + 1) * 2 * BLK)
                copies.append(
                    pltpu.make_async_copy(stage.at[which, :, window], outs[which].at[:, window], sems.at[which, at // 2])
                )
                copies[-1].start()
    for copy in copies:
        copy.wait()


def local(inputs, encoder_in, encoder_out, readings, available, pattern, gain, load, retain, smooth, cotangent):
    traces, steps, features = inputs.shape
    rows = traces * steps
    sensors, blocks = readings.shape[2], available.shape[2]
    states = encoder_out.shape[1]
    axis, times = lax.axis_size("state"), lax.axis_size("tm")
    swap = [(i, i ^ 1) for i in range(axis)]

    work = 2 * rows * sensors * states
    both = struct((2, rows, BLK), BF16)

    def across(pieces):
        moved = {k: lax.ppermute(pieces[k - 1], "state", [(i, (i + 2 * k) % axis) for i in range(axis)]) for k in (1, 3, 2)}
        return [moved[k] for k in (1, 2, 3)]

    near = (
        inputs.reshape(rows, features), encoder_in, encoder_out, gain, available.transpose(0, 2, 1),
        readings.reshape(rows, sensors),
    )
    pulled_from = (load, cotangent.reshape(rows, sensors))
    table = pattern.T
    chips = axis // 2
    parts = (struct((chips, rows, BLK), F32), struct((chips, rows, BLK), BF16))
    load_weights, keep_b, send_b, *near = call(
        pull_kernel,
        (struct((states, sensors), BF16), *parts, *(struct(a.shape, a.dtype) for a in near)),
        (table, *pulled_from, *near),
        scratch=[pltpu.SMEM(table.shape, table.dtype)]
        + [pltpu.VMEM(a.shape, a.dtype) for a in pulled_from]
        + [pltpu.SemaphoreType.DMA((9,))],
        hbm=9,
        flops=work,
    )
    came_b = lax.ppermute(send_b, "state", swap)
    gain_weights, keep_a, send_a, mask = call(
        drive_kernel,
        (struct((sensors, states), BF16), *parts, struct((rows, blocks), F32)),
        (*near, table),
        scratch=[
            pltpu.VMEM((rows, sensors), BF16),
            pltpu.SMEM(table.shape, table.dtype),
            pltpu.SemaphoreType.DMA,
        ],
        hbm=1,
        flops=work,
    )
    came_a = lax.ppermute(send_a, "state", swap)
    full, segments = struct((rows, BLK), F32), struct((traces, SEG, BLK), F32)
    keep_r, keep_s, root, ahead_p, filt_p, rise_p, fall_p, seg_r, seg_s = call(
        functools.partial(decay_kernel, traces, steps),
        (full,) * 7 + (segments,) * 2,
        (retain.reshape(-1, steps), smooth.reshape(-1, steps)),
    )
    decays = (keep_r, keep_s, root, ahead_p, filt_p, rise_p, fall_p, seg_r, seg_s)
    keep_a, decays = lax.optimization_barrier((keep_a, decays))
    keep_r, keep_s, root, ahead_p, filt_p, rise_p, fall_p, seg_r, seg_s = decays
    both = struct((2, rows, BLK), BF16)
    own, *sums = call(
        merge_kernel, (struct(both.shape, F32),) + (both,) * 3, (keep_a, keep_b, came_a, came_b)
    )
    sums = across(sums)
    scanned, pulled, before, parcel = call(
        functools.partial(scan_kernel, traces, steps),
        (full, full, struct((4, traces, 2, SEG, BLK), F32), struct((times, 2 * SEG, BLK), F32)),
        (own, *sums, keep_r, keep_s, root, seg_r, seg_s),
        scratch=[pltpu.VMEM((rows, BLK), F32)] * 2 + [pltpu.VMEM((2, 2, SEG, BLK), F32)],
    )
    parcel = lax.all_to_all(parcel, "tm", 0, 0)
    (smoothed,) = call(
        functools.partial(settle_kernel, traces, steps),
        (both,),
        (parcel, before, scanned, pulled, root, ahead_p, filt_p, rise_p, fall_p),
        scratch=[pltpu.VMEM((2, rows, BLK), F32), pltpu.VMEM((2, SEG, BLK), F32)],
    )
    same = [smoothed, *across([smoothed] * 3)]
    totals = ()
    for shift in (0, 1, 3, 2):
        last = shift == 2
        if shift == 1:
            totals, same[1] = lax.optimization_barrier((totals, same[1]))
            totals, same[3] = lax.optimization_barrier((totals, same[3]))
        if shift == 3:
            totals, same[2] = lax.optimization_barrier((totals, same[2]))
        partner = lax.ppermute(same[shift], "state", swap)
        totals = call(
            functools.partial(project_kernel, shift, last),
            (struct((rows, sensors), BF16 if last else F32),) * 2,
            (same[shift], partner, load_weights, gain_weights, mask, *totals),
            scratch=[pltpu.VMEM((2, rows, 2 * BLK), BF16)]
            + ([pltpu.VMEM((2, rows, sensors), BF16), pltpu.SemaphoreType.DMA((2, 2))] if last else []),
                hbm_out=last,
            flops=work // 2,
        )
    predicted, sensor_grad = totals
    return predicted.reshape(readings.shape), sensor_grad.reshape(readings.shape)


def solution(mesh):
    placed = (
        P(None, "tm", None),
        P(None, "state"),
        P("state", None),
        P(None, "tm", "state"),
        P(None, "tm", "state"),
        P("state", None),
        P("state", None, None, None),
        P("state", None, None, None),
        P("state", None, "tm"),
        P("state", None, "tm"),
        P(None, "tm", "state"),
    )
    return jax.shard_map(
        local,
        mesh=mesh,
        in_specs=placed,
        out_specs=(P(None, "tm", "state"), P(None, "tm", "state")),
        check_vma=False,
    )
```

```python
import functools

import jax
import jax.numpy as jnp
from jax import lax
from jax.experimental import pallas as pl
from jax.experimental.pallas import tpu as pltpu
from jax.sharding import PartitionSpec as P


F32, BF16 = jnp.float32, jnp.bfloat16
VMEM = 20 << 20
BLK = 128
SEG = 8
NT = (((1,), (1,)), ((), ()))
NN = (((1,), (0,)), ((), ()))


def call(kernel, outs, operands, scratch=(), hbm=0, hbm_out=False, flops=0, alias=None):
    vmem = pl.BlockSpec(memory_space=pltpu.VMEM)
    far = pl.BlockSpec(memory_space=pltpu.HBM)
    moved = sum(a.size * a.dtype.itemsize for a in (*operands, *outs))
    return pl.pallas_call(
        kernel,
        out_shape=outs,
        in_specs=[vmem] * (len(operands) - hbm) + [far] * hbm,
        out_specs=tuple([far if hbm_out else vmem] * len(outs)),
        scratch_shapes=list(scratch),
        input_output_aliases=alias or {},
        compiler_params=pltpu.CompilerParams(vmem_limit_bytes=VMEM),
        cost_estimate=pl.CostEstimate(flops=flops, bytes_accessed=moved, transcendentals=0),
    )(*operands[: len(operands) - hbm], *[in_hbm(a) for a in operands[len(operands) - hbm :]])


def in_hbm(array):
    return pltpu.with_memory_space_constraint(array, pltpu.HBM)


def struct(shape, dtype):
    return jax.ShapeDtypeStruct(shape, dtype)


def here():
    at = lax.axis_index("state")
    return lax.div(at, 2), lax.rem(at, 2)


def split(keep, send, at, total):
    mine = here()[1] == 0
    low, high = total[:, :BLK], total[:, BLK:]
    keep[at] = jnp.where(mine, low, high)
    send[at] = jnp.where(mine, high, low).astype(BF16)


def window_of(at):
    return slice(at * 2 * BLK, (at + 1) * 2 * BLK)


def pull_kernel(
    table_far, load_far, rows_far, enc_in_far, cot_far, enc_out_far, gain_far, available_far, readings_far,
    weights, keep, send, gain_weights, hidden, enc_out, gain, available, readings,
    pattern, load, rows_in, enc_in, cotangent, sems,
):
    pairs = (
        (table_far, pattern), (load_far, load), (rows_far, rows_in), (enc_in_far, enc_in), (cot_far, cotangent),
        (enc_out_far, enc_out), (gain_far, gain), (available_far, available), (readings_far, readings),
    )
    copies = [pltpu.make_async_copy(far, near, sems.at[i]) for i, (far, near) in enumerate(pairs)]
    for copy in copies[:5]:
        copy.start()
    weights[...] = jnp.zeros_like(weights)
    copies[0].wait()
    copies[1].wait()
    for copy in copies[5:]:
        copy.start()
    for q in range(load.shape[0]):
        for k in range(load.shape[1]):
            row = pl.multiple_of(pattern[k, q] * BLK, BLK)
            weights[pl.ds(row, BLK), q * BLK : (q + 1) * BLK] = load[q, k]
    copies[2].wait()
    copies[3].wait()
    hidden[...] = jax.nn.gelu(jnp.dot(rows_in[...], enc_in[...], preferred_element_type=F32)).astype(BF16)
    gain_weights[...] = jnp.zeros_like(gain_weights)
    copies[4].wait()
    for at in range(keep.shape[0]):
        total = lax.dot_general(cotangent[...], weights[window_of(at), :], NT, preferred_element_type=F32)
        split(keep, send, at, total)
    for copy in copies[5:]:
        copy.wait()


def drive_kernel(
    cleared, hidden, enc_out, gain, available, readings, table_far,
    weights, keep, send, mask,
    lhs, pattern, sem,
):
    fetch = pltpu.make_async_copy(table_far, pattern, sem)
    fetch.start()
    traces, blocks, steps = available.shape
    for b in range(traces):
        mask[b * steps : (b + 1) * steps, :] = available[b].astype(F32).T
    for q in range(blocks):
        lhs[:, q * BLK : (q + 1) * BLK] = readings[:, q * BLK : (q + 1) * BLK] * mask[:, q : q + 1].astype(BF16)
    fetch.wait()
    for q in range(blocks):
        for k in range(gain.shape[1]):
            column = pl.multiple_of(pattern[k, q] * BLK, BLK)
            weights[q * BLK : (q + 1) * BLK, pl.ds(column, BLK)] = gain[q, k]
    for at in range(keep.shape[0]):
        total = jnp.dot(lhs[...], weights[:, window_of(at)], preferred_element_type=F32)
        total += jnp.dot(hidden[...], enc_out[:, window_of(at)], preferred_element_type=F32)
        split(keep, send, at, total)


def merge_kernel(keep, came, own, *pieces):
    x, _ = here()
    for k, piece in enumerate((own, *pieces)):
        at = lax.rem(x + k, keep.shape[0])
        piece[...] = (keep[at] + came[at].astype(F32)).astype(piece.dtype)


def rows_of(b, u, steps):
    return pl.ds(b * steps + u, SEG, stride=steps // SEG)


def turn(x, by, fill, backward):
    row = lax.broadcasted_iota(jnp.int32, x.shape, 0)
    if backward:
        return jnp.where(row < SEG - by, pltpu.roll(x, SEG - by, 0), fill)
    return jnp.where(row >= by, pltpu.roll(x, by, 0), fill)


def chain(factor, value, backward):
    for by in (1, 2, 4):
        value = factor * turn(value, by, 0.0, backward) + value
        factor = factor * turn(factor, by, 1.0, backward)
    return factor, value, turn(factor, 1, 1.0, backward), turn(value, 1, 0.0, backward)


def decay_kernel(traces, steps, retain, smooth, keep_r, keep_s, root, ahead_p, filt_p, rise_p, fall_p, seg_r, seg_s):
    for b in range(traces):
        span = slice(b * steps, (b + 1) * steps)
        keep_r[span, :] = retain[pl.ds(b, BLK, stride=traces), :].T
        keep_s[span, :] = smooth[pl.ds(b, BLK, stride=traces), :].T
    root[...] = jnp.sqrt(1.0 - keep_r[...] * keep_r[...])
    ones = jnp.ones((SEG, BLK), F32)
    for b in range(traces):
        filt, rise = ones, ones
        for u in range(steps // SEG):
            at = rows_of(b, u, steps)
            r, s = keep_r[at, :], keep_s[at, :]
            filt = filt * r
            filt_p[at, :] = filt
            rise_p[at, :] = rise
            rise = rise * s
        seg_r[b] = filt
        seg_s[b] = rise
        ahead, fall = ones, ones
        for u in reversed(range(steps // SEG)):
            at = rows_of(b, u, steps)
            r, s = keep_r[at, :], keep_s[at, :]
            ahead = ahead * s
            ahead_p[at, :] = ahead
            fall_p[at, :] = fall
            fall = fall * r


def scan_kernel(
    traces, steps,
    own_a, own_b, a1, a2, a3, b1, b2, b3, keep_r, keep_s, root, seg_r, seg_s,
    states, grads, before, parcel,
    source, pull, ends,
):
    source[...] = root[...] * (own_a[...] + a1[...].astype(F32) + a2[...].astype(F32) + a3[...].astype(F32))
    pull[...] = own_b[...] + b1[...].astype(F32) + b2[...].astype(F32) + b3[...].astype(F32)
    for b in range(traces):
        filt = jnp.zeros((SEG, BLK), F32)
        rise, ahead, fall = filt, filt, filt
        for u in range(steps // SEG):
            at = rows_of(b, u, steps)
            r, s, g, p = keep_r[at, :], keep_s[at, :], source[at, :], pull[at, :]
            filt = r * filt + g
            states[at, :] = filt
            carried = rise + p
            grads[at, :] = carried
            rise = s * carried
        for u in reversed(range(steps // SEG)):
            at = rows_of(b, u, steps)
            r, s, g, p = keep_r[at, :], keep_s[at, :], source[at, :], pull[at, :]
            later = s * ahead
            states[at, :] = states[at, :] + later
            ahead = later + g
            grads[at, :] = grads[at, :] + fall
            fall = r * (fall + p)
        for which, (factor, value, backward) in enumerate(
            ((seg_r[b], filt, False), (seg_s[b], rise, False), (seg_s[b], ahead, True), (seg_r[b], fall, True))
        ):
            whole, total, factor_before, value_before = chain(factor, value, backward)
            before[which, b, 0] = factor_before
            before[which, b, 1] = value_before
            end = 0 if backward else SEG - 1
            half, row = which // 2, (which % 2) * traces + b
            ends[half, 0, row : row + 1, :] = total[end : end + 1, :]
            ends[half, 1, row : row + 1, :] = whole[end : end + 1, :]
    me = lax.axis_index("tm")
    for target in range(parcel.shape[0]):
        onward = target > me
        parcel[target, :SEG] = jnp.where(onward, ends[0, 0], ends[1, 0])
        parcel[target, SEG:] = jnp.where(onward, ends[0, 1], ends[1, 1])


def settle_kernel(
    traces, steps,
    parcel, before, states, grads, root, ahead_p, filt_p, rise_p, fall_p,
    smoothed,
    sums, carry,
):
    me, length = lax.axis_index("tm"), parcel.shape[0]
    onward = jnp.zeros((SEG, BLK), F32)
    back = onward
    for j in range(length):
        onward = jnp.where(j < me, parcel[j, SEG:] * onward + parcel[j, :SEG], onward)
        i = length - 1 - j
        back = jnp.where(i > me, parcel[i, SEG:] * back + parcel[i, :SEG], back)
    carry[0] = onward
    carry[1] = back
    for b in range(traces):
        filt, rise, ahead, fall = (
            before[w, b, 1] + before[w, b, 0] * carry[w // 2, (w % 2) * traces + b : (w % 2) * traces + b + 1, :]
            for w in range(4)
        )
        for u in range(steps // SEG):
            at = rows_of(b, u, steps)
            sums[0, at, :] = states[at, :] + filt_p[at, :] * filt + ahead_p[at, :] * ahead
            sums[1, at, :] = root[at, :] * (grads[at, :] + rise_p[at, :] * rise + fall_p[at, :] * fall)
    smoothed[...] = sums[...].astype(BF16)


def project_kernel(shift, last, mine, partner, load_weights, gain_weights, mask, *refs):
    before, refs = ((), refs) if shift == 0 else (refs[:2], refs[2:])
    outs, lhs, *rest = refs[:2], *refs[2:]
    x, core = here()
    block = pl.multiple_of(2 * BLK * lax.rem(x - shift + 4, 4), 2 * BLK)
    states = pl.ds(block, 2 * BLK)
    copies = []
    for which in range(2):
        for side, piece in enumerate((mine, partner)):
            column = pl.multiple_of(BLK * (core if side == 0 else 1 - core), BLK)
            lhs[which, :, pl.ds(column, BLK)] = piece[which]
        for at in range(4):
            window = slice(at * 2 * BLK, (at + 1) * 2 * BLK)
            if which == 0:
                total = lax.dot_general(lhs[0], load_weights[states, window], NN, preferred_element_type=F32)
            else:
                total = lax.dot_general(lhs[1], gain_weights[window, states], NT, preferred_element_type=F32)
            if before:
                total = before[which][:, window] + total
            if not last:
                outs[which][:, window] = total
                continue
            stage, sems = rest
            for half in range(2):
                q = 2 * at + half
                piece = total[:, half * BLK : (half + 1) * BLK]
                if which == 1:
                    piece = piece * mask[:, q : q + 1]
                stage[which, :, q * BLK : (q + 1) * BLK] = piece.astype(BF16)
            if at % 2:
                window = slice((at - 1) * 2 * BLK, (at + 1) * 2 * BLK)
                copies.append(
                    pltpu.make_async_copy(stage.at[which, :, window], outs[which].at[:, window], sems.at[which, at // 2])
                )
                copies[-1].start()
    for copy in copies:
        copy.wait()


def local(inputs, encoder_in, encoder_out, readings, available, pattern, gain, load, retain, smooth, cotangent):
    traces, steps, features = inputs.shape
    rows = traces * steps
    sensors, blocks = readings.shape[2], available.shape[2]
    states = encoder_out.shape[1]
    axis, times = lax.axis_size("state"), lax.axis_size("tm")
    swap = [(i, i ^ 1) for i in range(axis)]

    work = 2 * rows * sensors * states
    both = struct((2, rows, BLK), BF16)

    def across(pieces):
        moved = {k: lax.ppermute(pieces[k - 1], "state", [(i, (i + 2 * k) % axis) for i in range(axis)]) for k in (1, 3, 2)}
        return [moved[k] for k in (1, 2, 3)]

    fetched = (encoder_out, gain, available.transpose(0, 2, 1), readings.reshape(rows, sensors))
    staged = (load, inputs.reshape(rows, features), encoder_in, cotangent.reshape(rows, sensors))
    table = pattern.T
    parts = (struct((axis // 2, rows, BLK), F32), struct((axis // 2, rows, BLK), BF16))
    load_weights, keep_b, send_b, cleared, hidden, *fetched = call(
        pull_kernel,
        (
            struct((states, sensors), BF16), *parts, struct((sensors, states), BF16),
            struct((rows, encoder_in.shape[1]), BF16), *(struct(a.shape, a.dtype) for a in fetched),
        ),
        (table, *staged, *fetched),
        scratch=[pltpu.SMEM(table.shape, table.dtype)]
        + [pltpu.VMEM(a.shape, a.dtype) for a in staged]
        + [pltpu.SemaphoreType.DMA((9,))],
        hbm=9,
        flops=work,
    )
    came_b = lax.ppermute(send_b, "state", swap)
    gain_weights, keep_a, send_a, mask = call(
        drive_kernel,
        (struct((sensors, states), BF16), *parts, struct((rows, blocks), F32)),
        (cleared, hidden, *fetched, table),
        scratch=[
            pltpu.VMEM((rows, sensors), BF16),
            pltpu.SMEM(table.shape, table.dtype),
            pltpu.SemaphoreType.DMA,
        ],
        hbm=1,
        flops=work,
        alias={0: 0},
    )
    came_a = lax.ppermute(send_a, "state", swap)
    piece = struct((rows, BLK), BF16)
    pieces = (struct((rows, BLK), F32),) + (piece,) * 3
    own_b, *sums_b = call(merge_kernel, pieces, (keep_b, came_b))
    sums_b = across(sums_b)
    keep_a, own_b = lax.optimization_barrier((keep_a, own_b))
    own_a, *sums_a = call(merge_kernel, pieces, (keep_a, came_a))
    sums_a = across(sums_a)
    full, segments = struct((rows, BLK), F32), struct((traces, SEG, BLK), F32)
    keep_r, keep_s, root, ahead_p, filt_p, rise_p, fall_p, seg_r, seg_s = call(
        functools.partial(decay_kernel, traces, steps),
        (full,) * 7 + (segments,) * 2,
        (retain.reshape(-1, steps), smooth.reshape(-1, steps)),
    )
    scanned, pulled, before, parcel = call(
        functools.partial(scan_kernel, traces, steps),
        (full, full, struct((4, traces, 2, SEG, BLK), F32), struct((times, 2 * SEG, BLK), F32)),
        (own_a, own_b, *sums_a, *sums_b, keep_r, keep_s, root, seg_r, seg_s),
        scratch=[pltpu.VMEM((rows, BLK), F32)] * 2 + [pltpu.VMEM((2, 2, SEG, BLK), F32)],
    )
    parcel = lax.all_to_all(parcel, "tm", 0, 0)
    (smoothed,) = call(
        functools.partial(settle_kernel, traces, steps),
        (both,),
        (parcel, before, scanned, pulled, root, ahead_p, filt_p, rise_p, fall_p),
        scratch=[pltpu.VMEM((2, rows, BLK), F32), pltpu.VMEM((2, SEG, BLK), F32)],
    )
    same = [smoothed, *across([smoothed] * 3)]
    totals = ()
    for shift in (0, 1, 3, 2):
        last = shift == 2
        if shift == 1:
            totals, same[1] = lax.optimization_barrier((totals, same[1]))
            totals, same[3] = lax.optimization_barrier((totals, same[3]))
        if shift == 3:
            totals, same[2] = lax.optimization_barrier((totals, same[2]))
        partner = lax.ppermute(same[shift], "state", swap)
        totals = call(
            functools.partial(project_kernel, shift, last),
            (struct((rows, sensors), BF16 if last else F32),) * 2,
            (same[shift], partner, load_weights, gain_weights, mask, *totals),
            scratch=[pltpu.VMEM((2, rows, 2 * BLK), BF16)]
            + ([pltpu.VMEM((2, rows, sensors), BF16), pltpu.SemaphoreType.DMA((2, 2))] if last else []),
                hbm_out=last,
            flops=work // 2,
        )
    predicted, sensor_grad = totals
    return predicted.reshape(readings.shape), sensor_grad.reshape(readings.shape)


def solution(mesh):
    placed = (
        P(None, "tm", None),
        P(None, "state"),
        P("state", None),
        P(None, "tm", "state"),
        P(None, "tm", "state"),
        P("state", None),
        P("state", None, None, None),
        P("state", None, None, None),
        P("state", None, "tm"),
        P("state", None, "tm"),
        P(None, "tm", "state"),
    )
    return jax.shard_map(
        local,
        mesh=mesh,
        in_specs=placed,
        out_specs=(P(None, "tm", "state"), P(None, "tm", "state")),
        check_vma=False,
    )
```

```python
import functools

import jax
import jax.numpy as jnp
from jax import lax
from jax.experimental import pallas as pl
from jax.experimental.pallas import tpu as pltpu
from jax.sharding import PartitionSpec as P


F32, BF16 = jnp.float32, jnp.bfloat16
VMEM = 20 << 20
BLK = 128
SEG = 8
NT = (((1,), (1,)), ((), ()))
NN = (((1,), (0,)), ((), ()))


def call(kernel, outs, operands, scratch=(), hbm=0, hbm_out=False, flops=0, alias=None):
    vmem = pl.BlockSpec(memory_space=pltpu.VMEM)
    far = pl.BlockSpec(memory_space=pltpu.HBM)
    moved = sum(a.size * a.dtype.itemsize for a in (*operands, *outs))
    return pl.pallas_call(
        kernel,
        out_shape=outs,
        in_specs=[vmem] * (len(operands) - hbm) + [far] * hbm,
        out_specs=tuple([far if hbm_out else vmem] * len(outs)),
        scratch_shapes=list(scratch),
        input_output_aliases=alias or {},
        compiler_params=pltpu.CompilerParams(vmem_limit_bytes=VMEM),
        cost_estimate=pl.CostEstimate(flops=flops, bytes_accessed=moved, transcendentals=0),
    )(*operands[: len(operands) - hbm], *[in_hbm(a) for a in operands[len(operands) - hbm :]])


def in_hbm(array):
    return pltpu.with_memory_space_constraint(array, pltpu.HBM)


def struct(shape, dtype):
    return jax.ShapeDtypeStruct(shape, dtype)


def here():
    at = lax.axis_index("state")
    return lax.div(at, 2), lax.rem(at, 2)


def split(keep, send, at, total):
    mine = here()[1] == 0
    low, high = total[:, :BLK], total[:, BLK:]
    keep[at] = jnp.where(mine, low, high)
    send[at] = jnp.where(mine, high, low).astype(BF16)


def window_of(at):
    return slice(at * 2 * BLK, (at + 1) * 2 * BLK)


def pull_kernel(
    table_far, load_far, cot_far, rows_far, enc_in_far, enc_out_far, gain_far, available_far, readings_far,
    weights, keep, send, gain_weights, rows_in, enc_in, enc_out, gain, available, readings,
    pattern, load, cotangent, sems,
):
    pairs = (
        (table_far, pattern), (load_far, load), (cot_far, cotangent), (rows_far, rows_in), (enc_in_far, enc_in),
        (enc_out_far, enc_out), (gain_far, gain), (available_far, available), (readings_far, readings),
    )
    copies = [pltpu.make_async_copy(far, near, sems.at[i]) for i, (far, near) in enumerate(pairs)]
    for copy in copies[:3]:
        copy.start()
    weights[...] = jnp.zeros_like(weights)
    gain_weights[...] = jnp.zeros_like(gain_weights)
    copies[0].wait()
    copies[1].wait()
    for copy in copies[3:]:
        copy.start()
    for q in range(load.shape[0]):
        for k in range(load.shape[1]):
            row = pl.multiple_of(pattern[k, q] * BLK, BLK)
            weights[pl.ds(row, BLK), q * BLK : (q + 1) * BLK] = load[q, k]
    copies[2].wait()
    for at in range(keep.shape[0]):
        total = lax.dot_general(cotangent[...], weights[window_of(at), :], NT, preferred_element_type=F32)
        split(keep, send, at, total)
    for copy in copies[3:]:
        copy.wait()


def drive_kernel(
    cleared, rows_in, enc_in, enc_out, gain, available, readings, table_far,
    weights, keep, send, mask,
    lhs, pattern, sem,
):
    fetch = pltpu.make_async_copy(table_far, pattern, sem)
    fetch.start()
    traces, blocks, steps = available.shape
    hidden = jax.nn.gelu(jnp.dot(rows_in[...], enc_in[...], preferred_element_type=F32)).astype(BF16)
    for b in range(traces):
        mask[b * steps : (b + 1) * steps, :] = available[b].astype(F32).T
    for q in range(blocks):
        lhs[:, q * BLK : (q + 1) * BLK] = readings[:, q * BLK : (q + 1) * BLK] * mask[:, q : q + 1].astype(BF16)
    fetch.wait()
    for q in range(blocks):
        for k in range(gain.shape[1]):
            column = pl.multiple_of(pattern[k, q] * BLK, BLK)
            weights[q * BLK : (q + 1) * BLK, pl.ds(column, BLK)] = gain[q, k]
    for at in range(keep.shape[0]):
        total = jnp.dot(lhs[...], weights[:, window_of(at)], preferred_element_type=F32)
        total += jnp.dot(hidden, enc_out[:, window_of(at)], preferred_element_type=F32)
        split(keep, send, at, total)


def merge_kernel(keep, came, own, *pieces):
    x, _ = here()
    for k, piece in enumerate((own, *pieces)):
        at = lax.rem(x + k, keep.shape[0])
        piece[...] = (keep[at] + came[at].astype(F32)).astype(piece.dtype)


def rows_of(b, u, steps):
    return pl.ds(b * steps + u, SEG, stride=steps // SEG)


def turn(x, by, fill, backward):
    row = lax.broadcasted_iota(jnp.int32, x.shape, 0)
    if backward:
        return jnp.where(row < SEG - by, pltpu.roll(x, SEG - by, 0), fill)
    return jnp.where(row >= by, pltpu.roll(x, by, 0), fill)


def chain(factor, value, backward):
    for by in (1, 2, 4):
        value = factor * turn(value, by, 0.0, backward) + value
        factor = factor * turn(factor, by, 1.0, backward)
    return factor, value, turn(factor, 1, 1.0, backward), turn(value, 1, 0.0, backward)


def decay_kernel(traces, steps, retain, smooth, keep_r, keep_s, root, ahead_p, filt_p, rise_p, fall_p, seg_r, seg_s):
    for b in range(traces):
        span = slice(b * steps, (b + 1) * steps)
        keep_r[span, :] = retain[pl.ds(b, BLK, stride=traces), :].T
        keep_s[span, :] = smooth[pl.ds(b, BLK, stride=traces), :].T
    root[...] = jnp.sqrt(1.0 - keep_r[...] * keep_r[...])
    ones = jnp.ones((SEG, BLK), F32)
    for b in range(traces):
        filt, rise = ones, ones
        for u in range(steps // SEG):
            at = rows_of(b, u, steps)
            r, s = keep_r[at, :], keep_s[at, :]
            filt = filt * r
            filt_p[at, :] = filt
            rise_p[at, :] = rise
            rise = rise * s
        seg_r[b] = filt
        seg_s[b] = rise
        ahead, fall = ones, ones
        for u in reversed(range(steps // SEG)):
            at = rows_of(b, u, steps)
            r, s = keep_r[at, :], keep_s[at, :]
            ahead = ahead * s
            ahead_p[at, :] = ahead
            fall_p[at, :] = fall
            fall = fall * r


def scan_kernel(
    traces, steps,
    own_a, own_b, a1, a2, a3, b1, b2, b3, keep_r, keep_s, root, seg_r, seg_s,
    states, grads, before, parcel,
    source, pull, ends,
):
    source[...] = root[...] * (own_a[...] + a1[...].astype(F32) + a2[...].astype(F32) + a3[...].astype(F32))
    pull[...] = own_b[...] + b1[...].astype(F32) + b2[...].astype(F32) + b3[...].astype(F32)
    for b in range(traces):
        filt = jnp.zeros((SEG, BLK), F32)
        rise, ahead, fall = filt, filt, filt
        for u in range(steps // SEG):
            at = rows_of(b, u, steps)
            r, s, g, p = keep_r[at, :], keep_s[at, :], source[at, :], pull[at, :]
            filt = r * filt + g
            states[at, :] = filt
            carried = rise + p
            grads[at, :] = carried
            rise = s * carried
        for u in reversed(range(steps // SEG)):
            at = rows_of(b, u, steps)
            r, s, g, p = keep_r[at, :], keep_s[at, :], source[at, :], pull[at, :]
            later = s * ahead
            states[at, :] = states[at, :] + later
            ahead = later + g
            grads[at, :] = grads[at, :] + fall
            fall = r * (fall + p)
        for which, (factor, value, backward) in enumerate(
            ((seg_r[b], filt, False), (seg_s[b], rise, False), (seg_s[b], ahead, True), (seg_r[b], fall, True))
        ):
            whole, total, factor_before, value_before = chain(factor, value, backward)
            before[which, b, 0] = factor_before
            before[which, b, 1] = value_before
            end = 0 if backward else SEG - 1
            half, row = which // 2, (which % 2) * traces + b
            ends[half, row : row + 1, :] = total[end : end + 1, :]
            ends[half, SEG + row : SEG + row + 1, :] = -jnp.log(jnp.maximum(whole[end : end + 1, :], 1e-37))
    me = lax.axis_index("tm")
    for target in range(parcel.shape[0]):
        parcel[target] = jnp.where(target > me, ends[0], ends[1]).astype(BF16)


def settle_kernel(
    traces, steps,
    parcel, before, states, grads, root, ahead_p, filt_p, rise_p, fall_p,
    smoothed,
    sums, carry,
):
    me, length = lax.axis_index("tm"), parcel.shape[0]
    onward = jnp.zeros((SEG, BLK), F32)
    back = onward

    def pair(j):
        both = parcel[j].astype(F32)
        return jnp.exp(-both[SEG:]), both[:SEG]

    pairs = [pair(j) for j in range(length)]
    for j in range(length):
        factor, value = pairs[j]
        onward = jnp.where(j < me, factor * onward + value, onward)
        i = length - 1 - j
        factor, value = pairs[i]
        back = jnp.where(i > me, factor * back + value, back)
    carry[0] = onward
    carry[1] = back
    for b in range(traces):
        filt, rise, ahead, fall = (
            before[w, b, 1] + before[w, b, 0] * carry[w // 2, (w % 2) * traces + b : (w % 2) * traces + b + 1, :]
            for w in range(4)
        )
        for u in range(steps // SEG):
            at = rows_of(b, u, steps)
            sums[0, at, :] = states[at, :] + filt_p[at, :] * filt + ahead_p[at, :] * ahead
            sums[1, at, :] = root[at, :] * (grads[at, :] + rise_p[at, :] * rise + fall_p[at, :] * fall)
    smoothed[...] = sums[...].astype(BF16)


def project_kernel(shift, last, mine, partner, load_weights, gain_weights, mask, *refs):
    before, refs = ((), refs) if shift == 0 else (refs[:2], refs[2:])
    outs, lhs, *rest = refs[:2], *refs[2:]
    x, core = here()
    block = pl.multiple_of(2 * BLK * lax.rem(x - shift + 4, 4), 2 * BLK)
    states = pl.ds(block, 2 * BLK)
    copies = []
    for which in range(2):
        for side, piece in enumerate((mine, partner)):
            column = pl.multiple_of(BLK * (core if side == 0 else 1 - core), BLK)
            lhs[which, :, pl.ds(column, BLK)] = piece[which]
        for at in range(4):
            window = slice(at * 2 * BLK, (at + 1) * 2 * BLK)
            if which == 0:
                total = lax.dot_general(lhs[0], load_weights[states, window], NN, preferred_element_type=F32)
            else:
                total = lax.dot_general(lhs[1], gain_weights[window, states], NT, preferred_element_type=F32)
            if before:
                total = before[which][:, window] + total
            if not last:
                outs[which][:, window] = total
                continue
            stage, sems = rest
            for half in range(2):
                q = 2 * at + half
                piece = total[:, half * BLK : (half + 1) * BLK]
                if which == 1:
                    piece = piece * mask[:, q : q + 1]
                stage[which, :, q * BLK : (q + 1) * BLK] = piece.astype(BF16)
            if which == 1 or at % 2:
                window = window if which == 1 else slice((at - 1) * 2 * BLK, (at + 1) * 2 * BLK)
                copies.append(
                    pltpu.make_async_copy(stage.at[which, :, window], outs[which].at[:, window], sems.at[which, at])
                )
                copies[-1].start()
    for copy in copies:
        copy.wait()


def local(inputs, encoder_in, encoder_out, readings, available, pattern, gain, load, retain, smooth, cotangent):
    traces, steps, features = inputs.shape
    rows = traces * steps
    sensors, blocks = readings.shape[2], available.shape[2]
    states = encoder_out.shape[1]
    axis, times = lax.axis_size("state"), lax.axis_size("tm")
    swap = [(i, i ^ 1) for i in range(axis)]

    work = 2 * rows * sensors * states
    both = struct((2, rows, BLK), BF16)

    def across(pieces):
        moved = {k: lax.ppermute(pieces[k - 1], "state", [(i, (i + 2 * k) % axis) for i in range(axis)]) for k in (1, 3, 2)}
        return [moved[k] for k in (1, 2, 3)]

    fetched = (
        inputs.reshape(rows, features), encoder_in, encoder_out, gain, available.transpose(0, 2, 1),
        readings.reshape(rows, sensors),
    )
    staged = (load, cotangent.reshape(rows, sensors))
    table = pattern.T
    parts = (struct((axis // 2, rows, BLK), F32), struct((axis // 2, rows, BLK), BF16))
    load_weights, keep_b, send_b, cleared, *fetched = call(
        pull_kernel,
        (
            struct((states, sensors), BF16), *parts, struct((sensors, states), BF16),
            *(struct(a.shape, a.dtype) for a in fetched),
        ),
        (table, *staged, *fetched),
        scratch=[pltpu.SMEM(table.shape, table.dtype)]
        + [pltpu.VMEM(a.shape, a.dtype) for a in staged]
        + [pltpu.SemaphoreType.DMA((9,))],
        hbm=9,
        flops=work,
    )
    came_b = lax.ppermute(send_b, "state", swap)
    gain_weights, keep_a, send_a, mask = call(
        drive_kernel,
        (struct((sensors, states), BF16), *parts, struct((rows, blocks), F32)),
        (cleared, *fetched, table),
        scratch=[
            pltpu.VMEM((rows, sensors), BF16),
            pltpu.SMEM(table.shape, table.dtype),
            pltpu.SemaphoreType.DMA,
        ],
        hbm=1,
        flops=work,
        alias={0: 0},
    )
    came_a = lax.ppermute(send_a, "state", swap)
    piece = struct((rows, BLK), BF16)
    pieces = (struct((rows, BLK), F32),) + (piece,) * 3
    own_b, *sums_b = call(merge_kernel, pieces, (keep_b, came_b))
    sums_b = across(sums_b)
    keep_a, own_b = lax.optimization_barrier((keep_a, own_b))
    own_a, *sums_a = call(merge_kernel, pieces, (keep_a, came_a))
    sums_a = across(sums_a)
    full, segments = struct((rows, BLK), F32), struct((traces, SEG, BLK), F32)
    keep_r, keep_s, root, ahead_p, filt_p, rise_p, fall_p, seg_r, seg_s = call(
        functools.partial(decay_kernel, traces, steps),
        (full,) * 7 + (segments,) * 2,
        (retain.reshape(-1, steps), smooth.reshape(-1, steps)),
    )
    scanned, pulled, before, parcel = call(
        functools.partial(scan_kernel, traces, steps),
        (full, full, struct((4, traces, 2, SEG, BLK), F32), struct((times, 2 * SEG, BLK), BF16)),
        (own_a, own_b, *sums_a, *sums_b, keep_r, keep_s, root, seg_r, seg_s),
        scratch=[pltpu.VMEM((rows, BLK), F32)] * 2 + [pltpu.VMEM((2, 2 * SEG, BLK), F32)],
    )
    parcel = lax.all_to_all(parcel, "tm", 0, 0)
    (smoothed,) = call(
        functools.partial(settle_kernel, traces, steps),
        (both,),
        (parcel, before, scanned, pulled, root, ahead_p, filt_p, rise_p, fall_p),
        scratch=[pltpu.VMEM((2, rows, BLK), F32), pltpu.VMEM((2, SEG, BLK), F32)],
    )
    same = [smoothed, *across([smoothed] * 3)]
    totals = ()
    for shift in (0, 1, 3, 2):
        last = shift == 2
        if shift == 1:
            totals, same[1] = lax.optimization_barrier((totals, same[1]))
            totals, same[3] = lax.optimization_barrier((totals, same[3]))
        if shift == 3:
            totals, same[2] = lax.optimization_barrier((totals, same[2]))
        partner = lax.ppermute(same[shift], "state", swap)
        totals = call(
            functools.partial(project_kernel, shift, last),
            (struct((rows, sensors), BF16 if last else F32),) * 2,
            (same[shift], partner, load_weights, gain_weights, mask, *totals),
            scratch=[pltpu.VMEM((2, rows, 2 * BLK), BF16)]
            + ([pltpu.VMEM((2, rows, sensors), BF16), pltpu.SemaphoreType.DMA((2, 4))] if last else []),
                hbm_out=last,
            flops=work // 2,
        )
    predicted, sensor_grad = totals
    return predicted.reshape(readings.shape), sensor_grad.reshape(readings.shape)


def solution(mesh):
    placed = (
        P(None, "tm", None),
        P(None, "state"),
        P("state", None),
        P(None, "tm", "state"),
        P(None, "tm", "state"),
        P("state", None),
        P("state", None, None, None),
        P("state", None, None, None),
        P("state", None, "tm"),
        P("state", None, "tm"),
        P(None, "tm", "state"),
    )
    return jax.shard_map(
        local,
        mesh=mesh,
        in_specs=placed,
        out_specs=(P(None, "tm", "state"), P(None, "tm", "state")),
        check_vma=False,
    )
```

```python
import functools

import jax
import jax.numpy as jnp
from jax import lax
from jax.experimental import pallas as pl
from jax.experimental.pallas import tpu as pltpu
from jax.sharding import PartitionSpec as P


F32, BF16 = jnp.float32, jnp.bfloat16
VMEM = 20 << 20
BLK = 128
SEG = 8
NT = (((1,), (1,)), ((), ()))
NN = (((1,), (0,)), ((), ()))


def call(kernel, outs, operands, scratch=(), hbm=0, hbm_out=False, flops=0, alias=None):
    vmem = pl.BlockSpec(memory_space=pltpu.VMEM)
    far = pl.BlockSpec(memory_space=pltpu.HBM)
    moved = sum(a.size * a.dtype.itemsize for a in (*operands, *outs))
    return pl.pallas_call(
        kernel,
        out_shape=outs,
        in_specs=[vmem] * (len(operands) - hbm) + [far] * hbm,
        out_specs=tuple([far if hbm_out else vmem] * len(outs)),
        scratch_shapes=list(scratch),
        input_output_aliases=alias or {},
        compiler_params=pltpu.CompilerParams(vmem_limit_bytes=VMEM),
        cost_estimate=pl.CostEstimate(flops=flops, bytes_accessed=moved, transcendentals=0),
    )(*operands[: len(operands) - hbm], *[in_hbm(a) for a in operands[len(operands) - hbm :]])


def in_hbm(array):
    return pltpu.with_memory_space_constraint(array, pltpu.HBM)


def struct(shape, dtype):
    return jax.ShapeDtypeStruct(shape, dtype)


def here():
    at = lax.axis_index("state")
    return lax.div(at, 2), lax.rem(at, 2)


def split(keep, send, at, total):
    mine = here()[1] == 0
    low, high = total[:, :BLK], total[:, BLK:]
    keep[at] = jnp.where(mine, low, high)
    send[at] = jnp.where(mine, high, low).astype(BF16)


def window_of(at):
    return slice(at * 2 * BLK, (at + 1) * 2 * BLK)


def pull_kernel(
    table_far, load_far, cot_far, rows_far, enc_in_far, enc_out_far, gain_far, available_far, readings_far,
    weights, keep, send, gain_weights, rows_in, enc_in, enc_out, gain, available, readings,
    pattern, load, cotangent, sems,
):
    pairs = (
        (table_far, pattern), (load_far, load), (cot_far, cotangent), (rows_far, rows_in), (enc_in_far, enc_in),
        (enc_out_far, enc_out), (gain_far, gain), (available_far, available), (readings_far, readings),
    )
    copies = [pltpu.make_async_copy(far, near, sems.at[i]) for i, (far, near) in enumerate(pairs)]
    for copy in copies:
        copy.start()
    weights[...] = jnp.zeros_like(weights)
    gain_weights[...] = jnp.zeros_like(gain_weights)
    copies[0].wait()
    copies[1].wait()
    for q in range(load.shape[0]):
        for k in range(load.shape[1]):
            row = pl.multiple_of(pattern[k, q] * BLK, BLK)
            weights[pl.ds(row, BLK), q * BLK : (q + 1) * BLK] = load[q, k]
    copies[2].wait()
    for at in range(keep.shape[0]):
        total = lax.dot_general(cotangent[...], weights[window_of(at), :], NT, preferred_element_type=F32)
        split(keep, send, at, total)
    for copy in copies[3:]:
        copy.wait()


def drive_kernel(
    cleared, rows_in, enc_in, enc_out, gain, available, readings, table_far,
    weights, keep, send, mask,
    lhs, pattern, sem,
):
    fetch = pltpu.make_async_copy(table_far, pattern, sem)
    fetch.start()
    traces, blocks, steps = available.shape
    hidden = jax.nn.gelu(jnp.dot(rows_in[...], enc_in[...], preferred_element_type=F32)).astype(BF16)
    for b in range(traces):
        mask[b * steps : (b + 1) * steps, :] = available[b].astype(F32).T
    for q in range(blocks):
        lhs[:, q * BLK : (q + 1) * BLK] = readings[:, q * BLK : (q + 1) * BLK] * mask[:, q : q + 1].astype(BF16)
    fetch.wait()
    for q in range(blocks):
        for k in range(gain.shape[1]):
            column = pl.multiple_of(pattern[k, q] * BLK, BLK)
            weights[q * BLK : (q + 1) * BLK, pl.ds(column, BLK)] = gain[q, k]
    for at in range(keep.shape[0]):
        total = jnp.dot(lhs[...], weights[:, window_of(at)], preferred_element_type=F32)
        total += jnp.dot(hidden, enc_out[:, window_of(at)], preferred_element_type=F32)
        split(keep, send, at, total)


def merge_kernel(keep, came, own, *pieces):
    x, _ = here()
    for k, piece in enumerate((own, *pieces)):
        at = lax.rem(x + k, keep.shape[0])
        piece[...] = (keep[at] + came[at].astype(F32)).astype(piece.dtype)


def rows_of(b, u, steps):
    return pl.ds(b * steps + u, SEG, stride=steps // SEG)


def turn(x, by, fill, backward):
    row = lax.broadcasted_iota(jnp.int32, x.shape, 0)
    if backward:
        return jnp.where(row < SEG - by, pltpu.roll(x, SEG - by, 0), fill)
    return jnp.where(row >= by, pltpu.roll(x, by, 0), fill)


def chain(factor, value, backward):
    for by in (1, 2, 4):
        value = factor * turn(value, by, 0.0, backward) + value
        factor = factor * turn(factor, by, 1.0, backward)
    return factor, value, turn(factor, 1, 1.0, backward), turn(value, 1, 0.0, backward)


def decay_kernel(traces, steps, retain, smooth, keep_r, keep_s, root, ahead_p, filt_p, rise_p, fall_p, seg_r, seg_s):
    for b in range(traces):
        span = slice(b * steps, (b + 1) * steps)
        keep_r[span, :] = retain[pl.ds(b, BLK, stride=traces), :].T
        keep_s[span, :] = smooth[pl.ds(b, BLK, stride=traces), :].T
    root[...] = jnp.sqrt(1.0 - keep_r[...] * keep_r[...])
    ones = jnp.ones((SEG, BLK), F32)
    for b in range(traces):
        filt, rise = ones, ones
        for u in range(steps // SEG):
            at = rows_of(b, u, steps)
            r, s = keep_r[at, :], keep_s[at, :]
            filt = filt * r
            filt_p[at, :] = filt
            rise_p[at, :] = rise
            rise = rise * s
        seg_r[b] = filt
        seg_s[b] = rise
        ahead, fall = ones, ones
        for u in reversed(range(steps // SEG)):
            at = rows_of(b, u, steps)
            r, s = keep_r[at, :], keep_s[at, :]
            ahead = ahead * s
            ahead_p[at, :] = ahead
            fall_p[at, :] = fall
            fall = fall * r


def scan_kernel(
    traces, steps,
    own_a, own_b, a1, a2, a3, b1, b2, b3, keep_r, keep_s, root, seg_r, seg_s,
    states, grads, before, parcel,
    source, pull, ends,
):
    source[...] = root[...] * (own_a[...] + a1[...].astype(F32) + a2[...].astype(F32) + a3[...].astype(F32))
    pull[...] = own_b[...] + b1[...].astype(F32) + b2[...].astype(F32) + b3[...].astype(F32)
    for b in range(traces):
        filt = jnp.zeros((SEG, BLK), F32)
        rise, ahead, fall = filt, filt, filt
        for u in range(steps // SEG):
            at = rows_of(b, u, steps)
            r, s, g, p = keep_r[at, :], keep_s[at, :], source[at, :], pull[at, :]
            filt = r * filt + g
            states[at, :] = filt
            carried = rise + p
            grads[at, :] = carried
            rise = s * carried
        for u in reversed(range(steps // SEG)):
            at = rows_of(b, u, steps)
            r, s, g, p = keep_r[at, :], keep_s[at, :], source[at, :], pull[at, :]
            later = s * ahead
            states[at, :] = states[at, :] + later
            ahead = later + g
            grads[at, :] = grads[at, :] + fall
            fall = r * (fall + p)
        for which, (factor, value, backward) in enumerate(
            ((seg_r[b], filt, False), (seg_s[b], rise, False), (seg_s[b], ahead, True), (seg_r[b], fall, True))
        ):
            whole, total, factor_before, value_before = chain(factor, value, backward)
            before[which, b, 0] = factor_before
            before[which, b, 1] = value_before
            end = 0 if backward else SEG - 1
            half, row = which // 2, (which % 2) * traces + b
            ends[half, row : row + 1, :] = total[end : end + 1, :]
            ends[half, SEG + row : SEG + row + 1, :] = -jnp.log(jnp.maximum(whole[end : end + 1, :], 1e-37))
    me = lax.axis_index("tm")
    for target in range(parcel.shape[0]):
        parcel[target] = jnp.where(target > me, ends[0], ends[1]).astype(BF16)


def settle_kernel(
    traces, steps,
    parcel, before, states, grads, root, ahead_p, filt_p, rise_p, fall_p,
    smoothed,
    sums, carry,
):
    me, length = lax.axis_index("tm"), parcel.shape[0]
    onward = jnp.zeros((SEG, BLK), F32)
    back = onward

    def pair(j):
        both = parcel[j].astype(F32)
        return jnp.exp(-both[SEG:]), both[:SEG]

    pairs = [pair(j) for j in range(length)]
    for j in range(length):
        factor, value = pairs[j]
        onward = jnp.where(j < me, factor * onward + value, onward)
        i = length - 1 - j
        factor, value = pairs[i]
        back = jnp.where(i > me, factor * back + value, back)
    carry[0] = onward
    carry[1] = back
    for b in range(traces):
        filt, rise, ahead, fall = (
            before[w, b, 1] + before[w, b, 0] * carry[w // 2, (w % 2) * traces + b : (w % 2) * traces + b + 1, :]
            for w in range(4)
        )
        for u in range(steps // SEG):
            at = rows_of(b, u, steps)
            sums[0, at, :] = states[at, :] + filt_p[at, :] * filt + ahead_p[at, :] * ahead
            sums[1, at, :] = root[at, :] * (grads[at, :] + rise_p[at, :] * rise + fall_p[at, :] * fall)
    smoothed[...] = sums[...].astype(BF16)


def project_kernel(shift, last, mine, partner, load_weights, gain_weights, mask, *refs):
    before, refs = ((), refs) if shift == 0 else (refs[:2], refs[2:])
    outs, lhs, *rest = refs[:2], *refs[2:]
    x, core = here()
    block = pl.multiple_of(2 * BLK * lax.rem(x - shift + 4, 4), 2 * BLK)
    states = pl.ds(block, 2 * BLK)
    copies = []
    for which in range(2):
        for side, piece in enumerate((mine, partner)):
            column = pl.multiple_of(BLK * (core if side == 0 else 1 - core), BLK)
            lhs[which, :, pl.ds(column, BLK)] = piece[which]
        for at in range(4):
            window = slice(at * 2 * BLK, (at + 1) * 2 * BLK)
            if which == 0:
                total = lax.dot_general(lhs[0], load_weights[states, window], NN, preferred_element_type=F32)
            else:
                total = lax.dot_general(lhs[1], gain_weights[window, states], NT, preferred_element_type=F32)
            if before:
                total = before[which][:, window] + total
            if not last:
                outs[which][:, window] = total
                continue
            stage, sems = rest
            for half in range(2):
                q = 2 * at + half
                piece = total[:, half * BLK : (half + 1) * BLK]
                if which == 1:
                    piece = piece * mask[:, q : q + 1]
                stage[which, :, q * BLK : (q + 1) * BLK] = piece.astype(BF16)
            if at % 2:
                window = slice((at - 1) * 2 * BLK, (at + 1) * 2 * BLK)
                copies.append(
                    pltpu.make_async_copy(stage.at[which, :, window], outs[which].at[:, window], sems.at[which, at // 2])
                )
                copies[-1].start()
    for copy in copies:
        copy.wait()


def local(inputs, encoder_in, encoder_out, readings, available, pattern, gain, load, retain, smooth, cotangent):
    traces, steps, features = inputs.shape
    rows = traces * steps
    sensors, blocks = readings.shape[2], available.shape[2]
    states = encoder_out.shape[1]
    axis, times = lax.axis_size("state"), lax.axis_size("tm")
    swap = [(i, i ^ 1) for i in range(axis)]

    work = 2 * rows * sensors * states
    both = struct((2, rows, BLK), BF16)

    def across(pieces):
        moved = {}
        for k in (1, 3, 2):
            moved[k] = lax.ppermute(pieces[k - 1], "state", [(i, (i + 2 * k) % axis) for i in range(axis)])
        return [moved[k] for k in (1, 2, 3)]

    fetched = (
        inputs.reshape(rows, features), encoder_in, encoder_out, gain, available.transpose(0, 2, 1),
        readings.reshape(rows, sensors),
    )
    staged = (load, cotangent.reshape(rows, sensors))
    table = pattern.T
    parts = (struct((axis // 2, rows, BLK), F32), struct((axis // 2, rows, BLK), BF16))
    load_weights, keep_b, send_b, cleared, *fetched = call(
        pull_kernel,
        (
            struct((states, sensors), BF16), *parts, struct((sensors, states), BF16),
            *(struct(a.shape, a.dtype) for a in fetched),
        ),
        (table, *staged, *fetched),
        scratch=[pltpu.SMEM(table.shape, table.dtype)]
        + [pltpu.VMEM(a.shape, a.dtype) for a in staged]
        + [pltpu.SemaphoreType.DMA((9,))],
        hbm=9,
        flops=work,
    )
    came_b = lax.ppermute(send_b, "state", swap)
    gain_weights, keep_a, send_a, mask = call(
        drive_kernel,
        (struct((sensors, states), BF16), *parts, struct((rows, blocks), F32)),
        (cleared, *fetched, table),
        scratch=[
            pltpu.VMEM((rows, sensors), BF16),
            pltpu.SMEM(table.shape, table.dtype),
            pltpu.SemaphoreType.DMA,
        ],
        hbm=1,
        flops=work,
        alias={0: 0},
    )
    came_a = lax.ppermute(send_a, "state", swap)
    piece = struct((rows, BLK), BF16)
    pieces = (struct((rows, BLK), F32),) + (piece,) * 3
    own_b, *sums_b = call(merge_kernel, pieces, (keep_b, came_b))
    sums_b = across(sums_b)
    keep_a, own_b = lax.optimization_barrier((keep_a, own_b))
    own_a, *sums_a = call(merge_kernel, pieces, (keep_a, came_a))
    sums_a = across(sums_a)
    full, segments = struct((rows, BLK), F32), struct((traces, SEG, BLK), F32)
    keep_r, keep_s, root, ahead_p, filt_p, rise_p, fall_p, seg_r, seg_s = call(
        functools.partial(decay_kernel, traces, steps),
        (full,) * 7 + (segments,) * 2,
        (retain.reshape(-1, steps), smooth.reshape(-1, steps)),
    )
    scanned, pulled, before, parcel = call(
        functools.partial(scan_kernel, traces, steps),
        (full, full, struct((4, traces, 2, SEG, BLK), F32), struct((times, 2 * SEG, BLK), BF16)),
        (own_a, own_b, *sums_a, *sums_b, keep_r, keep_s, root, seg_r, seg_s),
        scratch=[pltpu.VMEM((rows, BLK), F32)] * 2 + [pltpu.VMEM((2, 2 * SEG, BLK), F32)],
    )
    parcel = lax.all_to_all(parcel, "tm", 0, 0)
    (smoothed,) = call(
        functools.partial(settle_kernel, traces, steps),
        (both,),
        (parcel, before, scanned, pulled, root, ahead_p, filt_p, rise_p, fall_p),
        scratch=[pltpu.VMEM((2, rows, BLK), F32), pltpu.VMEM((2, SEG, BLK), F32)],
    )
    same = [smoothed, *across([smoothed] * 3)]
    totals = ()
    for shift in (0, 1, 3, 2):
        last = shift == 2
        if shift == 1:
            totals, same[1] = lax.optimization_barrier((totals, same[1]))
            totals, same[3] = lax.optimization_barrier((totals, same[3]))
        if shift == 3:
            totals, same[2] = lax.optimization_barrier((totals, same[2]))
        partner = lax.ppermute(same[shift], "state", swap)
        totals = call(
            functools.partial(project_kernel, shift, last),
            (struct((rows, sensors), BF16 if last else F32),) * 2,
            (same[shift], partner, load_weights, gain_weights, mask, *totals),
            scratch=[pltpu.VMEM((2, rows, 2 * BLK), BF16)]
            + ([pltpu.VMEM((2, rows, sensors), BF16), pltpu.SemaphoreType.DMA((2, 2))] if last else []),
                hbm_out=last,
            flops=work // 2,
        )
    predicted, sensor_grad = totals
    return predicted.reshape(readings.shape), sensor_grad.reshape(readings.shape)


def solution(mesh):
    placed = (
        P(None, "tm", None),
        P(None, "state"),
        P("state", None),
        P(None, "tm", "state"),
        P(None, "tm", "state"),
        P("state", None),
        P("state", None, None, None),
        P("state", None, None, None),
        P("state", None, "tm"),
        P("state", None, "tm"),
        P(None, "tm", "state"),
    )
    return jax.shard_map(
        local,
        mesh=mesh,
        in_specs=placed,
        out_specs=(P(None, "tm", "state"), P(None, "tm", "state")),
        check_vma=False,
    )
```

```python
import functools

import jax
import jax.numpy as jnp
from jax import lax
from jax.experimental import pallas as pl
from jax.experimental.pallas import tpu as pltpu
from jax.sharding import PartitionSpec as P


F32, BF16 = jnp.float32, jnp.bfloat16
VMEM = 20 << 20
BLK = 128
SEG = 8
NT = (((1,), (1,)), ((), ()))
NN = (((1,), (0,)), ((), ()))


def call(kernel, outs, operands, scratch=(), hbm=0, hbm_out=False, flops=0, alias=None):
    vmem = pl.BlockSpec(memory_space=pltpu.VMEM)
    far = pl.BlockSpec(memory_space=pltpu.HBM)
    moved = sum(a.size * a.dtype.itemsize for a in (*operands, *outs))
    return pl.pallas_call(
        kernel,
        out_shape=outs,
        in_specs=[vmem] * (len(operands) - hbm) + [far] * hbm,
        out_specs=tuple([far if hbm_out else vmem] * len(outs)),
        scratch_shapes=list(scratch),
        input_output_aliases=alias or {},
        compiler_params=pltpu.CompilerParams(vmem_limit_bytes=VMEM),
        cost_estimate=pl.CostEstimate(flops=flops, bytes_accessed=moved, transcendentals=0),
    )(*operands[: len(operands) - hbm], *[in_hbm(a) for a in operands[len(operands) - hbm :]])


def in_hbm(array):
    return pltpu.with_memory_space_constraint(array, pltpu.HBM)


def struct(shape, dtype):
    return jax.ShapeDtypeStruct(shape, dtype)


def here():
    at = lax.axis_index("state")
    return lax.div(at, 2), lax.rem(at, 2)


def split(keep, send, at, total):
    mine = here()[1] == 0
    low, high = total[:, :BLK], total[:, BLK:]
    keep[at] = jnp.where(mine, low, high)
    send[at] = jnp.where(mine, high, low).astype(BF16)


def window_of(at):
    return slice(at * 2 * BLK, (at + 1) * 2 * BLK)


def pull_kernel(
    table_far, load_far, cot_far, rows_far, enc_in_far, enc_out_far, gain_far, available_far, readings_far,
    weights, keep, send, gain_weights, rows_in, enc_in, enc_out, gain, available, readings,
    pattern, load, cotangent, sems,
):
    pairs = (
        (table_far, pattern), (load_far, load), (cot_far, cotangent), (rows_far, rows_in), (enc_in_far, enc_in),
        (enc_out_far, enc_out), (gain_far, gain), (available_far, available), (readings_far, readings),
    )
    copies = [pltpu.make_async_copy(far, near, sems.at[i]) for i, (far, near) in enumerate(pairs)]
    for copy in copies:
        copy.start()
    weights[...] = jnp.zeros_like(weights)
    gain_weights[...] = jnp.zeros_like(gain_weights)
    copies[0].wait()
    copies[1].wait()
    for q in range(load.shape[0]):
        for k in range(load.shape[1]):
            row = pl.multiple_of(pattern[k, q] * BLK, BLK)
            weights[pl.ds(row, BLK), q * BLK : (q + 1) * BLK] = load[q, k]
    copies[2].wait()
    for at in range(keep.shape[0]):
        total = lax.dot_general(cotangent[...], weights[window_of(at), :], NT, preferred_element_type=F32)
        split(keep, send, at, total)
    for copy in copies[3:]:
        copy.wait()


def drive_kernel(
    cleared, rows_in, enc_in, enc_out, gain, available, readings, table_far,
    weights, keep, send, mask,
    lhs, pattern, sem,
):
    fetch = pltpu.make_async_copy(table_far, pattern, sem)
    fetch.start()
    traces, blocks, steps = available.shape
    hidden = jax.nn.gelu(jnp.dot(rows_in[...], enc_in[...], preferred_element_type=F32)).astype(BF16)
    for b in range(traces):
        mask[b * steps : (b + 1) * steps, :] = available[b].astype(F32).T
    for q in range(blocks):
        lhs[:, q * BLK : (q + 1) * BLK] = readings[:, q * BLK : (q + 1) * BLK] * mask[:, q : q + 1].astype(BF16)
    fetch.wait()
    for q in range(blocks):
        for k in range(gain.shape[1]):
            column = pl.multiple_of(pattern[k, q] * BLK, BLK)
            weights[q * BLK : (q + 1) * BLK, pl.ds(column, BLK)] = gain[q, k]
    for at in range(keep.shape[0]):
        total = jnp.dot(lhs[...], weights[:, window_of(at)], preferred_element_type=F32)
        total += jnp.dot(hidden, enc_out[:, window_of(at)], preferred_element_type=F32)
        split(keep, send, at, total)


def merge_kernel(keep, came, own, *pieces):
    x, _ = here()
    for k, piece in enumerate((own, *pieces)):
        at = lax.rem(x + k, keep.shape[0])
        piece[...] = (keep[at] + came[at].astype(F32)).astype(piece.dtype)


def rows_of(b, u, steps):
    return pl.ds(b * steps + u, SEG, stride=steps // SEG)


def turn(x, by, fill, backward):
    row = lax.broadcasted_iota(jnp.int32, x.shape, 0)
    if backward:
        return jnp.where(row < SEG - by, pltpu.roll(x, SEG - by, 0), fill)
    return jnp.where(row >= by, pltpu.roll(x, by, 0), fill)


def chain(factor, value, backward):
    for by in (1, 2, 4):
        value = factor * turn(value, by, 0.0, backward) + value
        factor = factor * turn(factor, by, 1.0, backward)
    return factor, value, turn(factor, 1, 1.0, backward), turn(value, 1, 0.0, backward)


def decay_kernel(traces, steps, retain, smooth, keep_r, keep_s, root, ahead_p, filt_p, rise_p, fall_p, seg_r, seg_s):
    for b in range(traces):
        span = slice(b * steps, (b + 1) * steps)
        keep_r[span, :] = retain[pl.ds(b, BLK, stride=traces), :].T
        keep_s[span, :] = smooth[pl.ds(b, BLK, stride=traces), :].T
    root[...] = jnp.sqrt(1.0 - keep_r[...] * keep_r[...])
    ones = jnp.ones((SEG, BLK), F32)
    for b in range(traces):
        filt, rise = ones, ones
        for u in range(steps // SEG):
            at = rows_of(b, u, steps)
            r, s = keep_r[at, :], keep_s[at, :]
            filt = filt * r
            filt_p[at, :] = filt
            rise_p[at, :] = rise
            rise = rise * s
        seg_r[b] = filt
        seg_s[b] = rise
        ahead, fall = ones, ones
        for u in reversed(range(steps // SEG)):
            at = rows_of(b, u, steps)
            r, s = keep_r[at, :], keep_s[at, :]
            ahead = ahead * s
            ahead_p[at, :] = ahead
            fall_p[at, :] = fall
            fall = fall * r


def scan_kernel(
    traces, steps,
    own_a, own_b, a1, a2, a3, b1, b2, b3, keep_r, keep_s, root, seg_r, seg_s,
    states, grads, before, parcel,
    source, pull, ends,
):
    source[...] = root[...] * (own_a[...] + a1[...].astype(F32) + a2[...].astype(F32) + a3[...].astype(F32))
    pull[...] = own_b[...] + b1[...].astype(F32) + b2[...].astype(F32) + b3[...].astype(F32)
    for b in range(traces):
        filt = jnp.zeros((SEG, BLK), F32)
        rise, ahead, fall = filt, filt, filt
        for u in range(steps // SEG):
            at = rows_of(b, u, steps)
            r, s, g, p = keep_r[at, :], keep_s[at, :], source[at, :], pull[at, :]
            filt = r * filt + g
            states[at, :] = filt
            carried = rise + p
            grads[at, :] = carried
            rise = s * carried
        for u in reversed(range(steps // SEG)):
            at = rows_of(b, u, steps)
            r, s, g, p = keep_r[at, :], keep_s[at, :], source[at, :], pull[at, :]
            later = s * ahead
            states[at, :] = states[at, :] + later
            ahead = later + g
            grads[at, :] = grads[at, :] + fall
            fall = r * (fall + p)
        for which, (factor, value, backward) in enumerate(
            ((seg_r[b], filt, False), (seg_s[b], rise, False), (seg_s[b], ahead, True), (seg_r[b], fall, True))
        ):
            whole, total, factor_before, value_before = chain(factor, value, backward)
            before[which, b, 0] = factor_before
            before[which, b, 1] = value_before
            end = 0 if backward else SEG - 1
            half, row = which // 2, (which % 2) * traces + b
            ends[half, row : row + 1, :] = total[end : end + 1, :]
            ends[half, SEG + row : SEG + row + 1, :] = -jnp.log(jnp.maximum(whole[end : end + 1, :], 1e-37))
    me = lax.axis_index("tm")
    for target in range(parcel.shape[0]):
        parcel[target] = jnp.where(target > me, ends[0], ends[1]).astype(BF16)


def settle_kernel(
    traces, steps,
    parcel, before, states, grads, root, ahead_p, filt_p, rise_p, fall_p,
    smoothed,
    sums, carry,
):
    me, length = lax.axis_index("tm"), parcel.shape[0]

    def pair(j):
        both = parcel[j].astype(F32)
        return jnp.exp(-both[SEG:]), both[:SEG]

    def tree(items):
        while len(items) > 1:
            odd = items[len(items) // 2 * 2 :]
            items = [
                (first[0] * then[0], then[0] * first[1] + then[1]) for first, then in zip(items[::2], items[1::2])
            ] + odd
        return items[0][1]

    pairs = [pair(j) for j in range(length)]
    onward = tree([(jnp.where(j < me, f, 1.0), jnp.where(j < me, v, 0.0)) for j, (f, v) in enumerate(pairs)])
    back = tree([(jnp.where(j > me, f, 1.0), jnp.where(j > me, v, 0.0)) for j, (f, v) in enumerate(pairs)][::-1])
    carry[0] = onward
    carry[1] = back
    for b in range(traces):
        filt, rise, ahead, fall = (
            before[w, b, 1] + before[w, b, 0] * carry[w // 2, (w % 2) * traces + b : (w % 2) * traces + b + 1, :]
            for w in range(4)
        )
        for u in range(steps // SEG):
            at = rows_of(b, u, steps)
            sums[0, at, :] = states[at, :] + filt_p[at, :] * filt + ahead_p[at, :] * ahead
            sums[1, at, :] = root[at, :] * (grads[at, :] + rise_p[at, :] * rise + fall_p[at, :] * fall)
    smoothed[...] = sums[...].astype(BF16)


def project_kernel(shift, last, mine, partner, load_weights, gain_weights, mask, *refs):
    before, refs = ((), refs) if shift == 0 else (refs[:2], refs[2:])
    outs, lhs, *rest = refs[:2], *refs[2:]
    x, core = here()
    block = pl.multiple_of(2 * BLK * lax.rem(x - shift + 4, 4), 2 * BLK)
    states = pl.ds(block, 2 * BLK)
    copies = []
    for which in range(2):
        for side, piece in enumerate((mine, partner)):
            column = pl.multiple_of(BLK * (core if side == 0 else 1 - core), BLK)
            lhs[which, :, pl.ds(column, BLK)] = piece[which]
        for at in range(4):
            window = slice(at * 2 * BLK, (at + 1) * 2 * BLK)
            if which == 0:
                total = lax.dot_general(lhs[0], load_weights[states, window], NN, preferred_element_type=F32)
            else:
                total = lax.dot_general(lhs[1], gain_weights[window, states], NT, preferred_element_type=F32)
            if before:
                total = before[which][:, window] + total
            if not last:
                outs[which][:, window] = total
                continue
            stage, sems = rest
            for half in range(2):
                q = 2 * at + half
                piece = total[:, half * BLK : (half + 1) * BLK]
                if which == 1:
                    piece = piece * mask[:, q : q + 1]
                stage[which, :, q * BLK : (q + 1) * BLK] = piece.astype(BF16)
            if at % 2:
                window = slice((at - 1) * 2 * BLK, (at + 1) * 2 * BLK)
                copies.append(
                    pltpu.make_async_copy(stage.at[which, :, window], outs[which].at[:, window], sems.at[which, at // 2])
                )
                copies[-1].start()
    for copy in copies:
        copy.wait()


def local(inputs, encoder_in, encoder_out, readings, available, pattern, gain, load, retain, smooth, cotangent):
    traces, steps, features = inputs.shape
    rows = traces * steps
    sensors, blocks = readings.shape[2], available.shape[2]
    states = encoder_out.shape[1]
    axis, times = lax.axis_size("state"), lax.axis_size("tm")
    swap = [(i, i ^ 1) for i in range(axis)]

    work = 2 * rows * sensors * states
    both = struct((2, rows, BLK), BF16)

    def across(pieces):
        moved = {}
        for k in (1, 3, 2):
            moved[k] = lax.ppermute(pieces[k - 1], "state", [(i, (i + 2 * k) % axis) for i in range(axis)])
        return [moved[k] for k in (1, 2, 3)]

    fetched = (
        inputs.reshape(rows, features), encoder_in, encoder_out, gain, available.transpose(0, 2, 1),
        readings.reshape(rows, sensors),
    )
    staged = (load, cotangent.reshape(rows, sensors))
    table = pattern.T
    parts = (struct((axis // 2, rows, BLK), F32), struct((axis // 2, rows, BLK), BF16))
    load_weights, keep_b, send_b, cleared, *fetched = call(
        pull_kernel,
        (
            struct((states, sensors), BF16), *parts, struct((sensors, states), BF16),
            *(struct(a.shape, a.dtype) for a in fetched),
        ),
        (table, *staged, *fetched),
        scratch=[pltpu.SMEM(table.shape, table.dtype)]
        + [pltpu.VMEM(a.shape, a.dtype) for a in staged]
        + [pltpu.SemaphoreType.DMA((9,))],
        hbm=9,
        flops=work,
    )
    came_b = lax.ppermute(send_b, "state", swap)
    gain_weights, keep_a, send_a, mask = call(
        drive_kernel,
        (struct((sensors, states), BF16), *parts, struct((rows, blocks), F32)),
        (cleared, *fetched, table),
        scratch=[
            pltpu.VMEM((rows, sensors), BF16),
            pltpu.SMEM(table.shape, table.dtype),
            pltpu.SemaphoreType.DMA,
        ],
        hbm=1,
        flops=work,
        alias={0: 0},
    )
    came_a = lax.ppermute(send_a, "state", swap)
    piece = struct((rows, BLK), BF16)
    pieces = (struct((rows, BLK), F32),) + (piece,) * 3
    own_b, *sums_b = call(merge_kernel, pieces, (keep_b, came_b))
    sums_b = across(sums_b)
    keep_a, own_b = lax.optimization_barrier((keep_a, own_b))
    own_a, *sums_a = call(merge_kernel, pieces, (keep_a, came_a))
    sums_a = across(sums_a)
    full, segments = struct((rows, BLK), F32), struct((traces, SEG, BLK), F32)
    keep_r, keep_s, root, ahead_p, filt_p, rise_p, fall_p, seg_r, seg_s = call(
        functools.partial(decay_kernel, traces, steps),
        (full,) * 7 + (segments,) * 2,
        (retain.reshape(-1, steps), smooth.reshape(-1, steps)),
    )
    scanned, pulled, before, parcel = call(
        functools.partial(scan_kernel, traces, steps),
        (full, full, struct((4, traces, 2, SEG, BLK), F32), struct((times, 2 * SEG, BLK), BF16)),
        (own_a, own_b, *sums_a, *sums_b, keep_r, keep_s, root, seg_r, seg_s),
        scratch=[pltpu.VMEM((rows, BLK), F32)] * 2 + [pltpu.VMEM((2, 2 * SEG, BLK), F32)],
    )
    parcel = lax.all_to_all(parcel, "tm", 0, 0)
    (smoothed,) = call(
        functools.partial(settle_kernel, traces, steps),
        (both,),
        (parcel, before, scanned, pulled, root, ahead_p, filt_p, rise_p, fall_p),
        scratch=[pltpu.VMEM((2, rows, BLK), F32), pltpu.VMEM((2, SEG, BLK), F32)],
    )
    same = [smoothed, *across([smoothed] * 3)]
    totals = ()
    for shift in (0, 1, 3, 2):
        last = shift == 2
        if shift == 1:
            totals, same[1] = lax.optimization_barrier((totals, same[1]))
            totals, same[3] = lax.optimization_barrier((totals, same[3]))
        if shift == 3:
            totals, same[2] = lax.optimization_barrier((totals, same[2]))
        partner = lax.ppermute(same[shift], "state", swap)
        totals = call(
            functools.partial(project_kernel, shift, last),
            (struct((rows, sensors), BF16 if last else F32),) * 2,
            (same[shift], partner, load_weights, gain_weights, mask, *totals),
            scratch=[pltpu.VMEM((2, rows, 2 * BLK), BF16)]
            + ([pltpu.VMEM((2, rows, sensors), BF16), pltpu.SemaphoreType.DMA((2, 2))] if last else []),
                hbm_out=last,
            flops=work // 2,
        )
    predicted, sensor_grad = totals
    return predicted.reshape(readings.shape), sensor_grad.reshape(readings.shape)


def solution(mesh):
    placed = (
        P(None, "tm", None),
        P(None, "state"),
        P("state", None),
        P(None, "tm", "state"),
        P(None, "tm", "state"),
        P("state", None),
        P("state", None, None, None),
        P("state", None, None, None),
        P("state", None, "tm"),
        P("state", None, "tm"),
        P(None, "tm", "state"),
    )
    return jax.shard_map(
        local,
        mesh=mesh,
        in_specs=placed,
        out_specs=(P(None, "tm", "state"), P(None, "tm", "state")),
        check_vma=False,
    )
```
